256 devices in a mesh: segment: 4 (over y_hi, core), ctx: 64 (over x, z, y_lo).
Axes of the slice: x: 4, y: 4 (y_hi: 2, y_lo: 2; y = y_hi * 2 + y_lo), z: 8, core: 2. Of those that a mesh axis runs over, the one named last changes fastest.
Arguments:
- saved_inputs: bfloat16 [4, 2, 8192, 2048], P('segment', None, 'ctx'), may hold values from -6 to 6
- scale_gains: float32 [4, 3, 2048], P('segment'), may hold values from 0.1 to 1.9
- out_proj: bfloat16 [4, 2048, 2048], P('segment'), may hold values from -0.125 to 0.125
- top_grad: bfloat16 [2, 8192, 2048], P(None, 'ctx'), may hold values from -6 to 6
Outputs:
- input_grads: bfloat16 [4, 2, 8192, 2048], P('segment', None, 'ctx')
The draws below stay inside these ranges and needn't reach their ends.
All inputs are finite; a program needn't handle non-finite values.
Results may differ from the reference program's by a relative error of at most 0.015.
Values may be sent and summed in bfloat16 or wider, within the bound.
A program may use at most 128 MiB of HBM per device.

```python
import jax
import jax.numpy as jnp
from jax import lax

HEADS = 16
HEAD_DIM = 128
MB = 2
SPAN = 2
TOK_DEV = 128
WINDOW = 256
TOKENS = 8192
SEGMENTS = 4
N_CTX = 64


def block_levels(stream_key, shape, pieces, low, top_value):
    level = 1.0
    for position, parts in pieces:
        heights = jax.random.uniform(jax.random.fold_in(jax.random.fold_in(stream_key, 6), position), (parts,), jnp.float32, low / len(pieces), top_value / len(pieces))
        level = level * jnp.repeat(jnp.exp(heights), shape[position] // parts).reshape((-1,) + (1,) * (len(shape) - 1 - position))
    return level


def noise(key, extent, spread, most, shards=(), held_as=jnp.bfloat16):
    values = jax.random.normal(key, extent, jnp.float32) * spread
    if len(shards) > 0:
        values = block_levels(key, extent, shards, -0.22, 0.18) * values
    return jnp.clip(values, min=-most, max=most).astype(held_as)


def setup_inputs(seed: int = 0) -> dict:
    key_of = jax.random.split(jax.random.key(seed), 5)
    return {
        "saved_inputs": noise(key_of[0], (SEGMENTS, MB, TOKENS, HEADS * HEAD_DIM), 1.0, 6.0, ((0, 4), (2, 64))),
        "scale_gains": jnp.clip(1.0 + 0.18 * jax.random.normal(key_of[1], (SEGMENTS, 3, HEADS * HEAD_DIM), jnp.float32), 0.1, 1.9),
        "out_proj": noise(key_of[2], (SEGMENTS, HEADS * HEAD_DIM, HEADS * HEAD_DIM), (HEADS * HEAD_DIM) ** -0.5, 0.125, ((0, 4),)),
        "top_grad": noise(key_of[3], (MB, TOKENS, HEADS * HEAD_DIM), 1.0, 6.0, ((1, 64),)),
    }


QUERY_SCALE = 1.0 / 12.0
SOFT_CAP = 50.0


def attend_grads(query_rows, grad_rows, key_all, value_all, query_pos, key_pos):
    query_f = query_rows.astype(jnp.float32)
    grad_f = grad_rows.astype(jnp.float32)
    key_f = key_all.astype(jnp.float32)
    value_f = value_all.astype(jnp.float32)
    scores = jnp.einsum("thd,khd->htk", query_f, key_f) * QUERY_SCALE
    tanh_part = jnp.tanh(scores / SOFT_CAP)
    visible = (key_pos[None, :] <= query_pos[:, None]) & (key_pos[None, :] > query_pos[:, None] - WINDOW) & (key_pos[None, :] >= 0)
    masked_exp = jnp.where(visible[None], jnp.exp(SOFT_CAP * tanh_part), 0.0)
    weights = masked_exp / jnp.sum(masked_exp, axis=2, keepdims=True)
    grad_weight = jnp.einsum("thd,khd->htk", grad_f, value_f)
    row_dot = jnp.sum(weights * grad_weight, axis=2, keepdims=True)
    dscore = (weights * (grad_weight - row_dot) * (1.0 - tanh_part * tanh_part) * QUERY_SCALE).astype(jnp.bfloat16)
    weight_b = weights.astype(jnp.bfloat16)
    grad_value = jnp.einsum("htk,thd->khd", weight_b.astype(jnp.float32), grad_f).astype(jnp.bfloat16)
    grad_query = jnp.einsum("htk,khd->thd", dscore.astype(jnp.float32), key_f)
    grad_key = jnp.einsum("htk,thd->khd", dscore.astype(jnp.float32), query_f).astype(jnp.bfloat16)
    return grad_query, grad_key, grad_value


def layer_backward(inputs, gain_rows, projection, grad_in):
    features = HEADS * HEAD_DIM
    input_f = inputs.astype(jnp.float32)
    query_rows = (input_f * gain_rows[0]).astype(jnp.bfloat16).reshape(TOKENS, HEADS, HEAD_DIM)
    key_rows = (input_f * gain_rows[1]).astype(jnp.bfloat16).reshape(TOKENS, HEADS, HEAD_DIM)
    value_rows = (input_f * gain_rows[2]).astype(jnp.bfloat16).reshape(TOKENS, HEADS, HEAD_DIM)
    head_grad = jnp.dot(grad_in, projection.T, preferred_element_type=jnp.float32).astype(jnp.bfloat16)
    grad_rows = head_grad.reshape(TOKENS, HEADS, HEAD_DIM)
    lead_rows = SPAN * TOK_DEV
    padding = jnp.zeros((lead_rows, HEADS, HEAD_DIM), jnp.bfloat16)
    key_pad = jnp.concatenate([padding, key_rows], axis=0)
    value_pad = jnp.concatenate([padding, value_rows], axis=0)

    def block_step(totals, block_at):
        key_total, value_total = totals
        begin_at = (block_at * TOK_DEV).astype(jnp.int32)
        query_blk = lax.dynamic_slice_in_dim(query_rows, begin_at, TOK_DEV, 0)
        grad_blk = lax.dynamic_slice_in_dim(grad_rows, begin_at, TOK_DEV, 0)
        key_blk = lax.dynamic_slice_in_dim(key_pad, begin_at, lead_rows + TOK_DEV, 0)
        value_blk = lax.dynamic_slice_in_dim(value_pad, begin_at, lead_rows + TOK_DEV, 0)
        query_pos = begin_at + jnp.arange(TOK_DEV, dtype=jnp.int32)
        key_pos = begin_at - lead_rows + jnp.arange(lead_rows + TOK_DEV, dtype=jnp.int32)
        grad_query, grad_key, grad_value = attend_grads(query_blk, grad_blk, key_blk, value_blk, query_pos, key_pos)
        old_key = lax.dynamic_slice_in_dim(key_total, begin_at, lead_rows + TOK_DEV, 0)
        old_value = lax.dynamic_slice_in_dim(value_total, begin_at, lead_rows + TOK_DEV, 0)
        key_total = lax.dynamic_update_slice_in_dim(key_total, old_key + grad_key.astype(jnp.float32), begin_at, 0)
        value_total = lax.dynamic_update_slice_in_dim(value_total, old_value + grad_value.astype(jnp.float32), begin_at, 0)
        return (key_total, value_total), grad_query

    start_totals = (jnp.zeros((lead_rows + TOKENS, HEADS, HEAD_DIM), jnp.float32), jnp.zeros((lead_rows + TOKENS, HEADS, HEAD_DIM), jnp.float32))
    (key_total, value_total), query_grads = lax.scan(block_step, start_totals, jnp.arange(N_CTX, dtype=jnp.int32))
    grad_query = query_grads.reshape(TOKENS, features)
    grad_key = key_total[lead_rows:].reshape(TOKENS, features)
    grad_value = value_total[lead_rows:].reshape(TOKENS, features)
    total = grad_in.astype(jnp.float32) + gain_rows[0] * grad_query + gain_rows[1] * grad_key + gain_rows[2] * grad_value
    return total.astype(jnp.bfloat16)


def reference(saved_inputs, scale_gains, out_proj, top_grad):
    result = jnp.zeros((SEGMENTS, MB, TOKENS, HEADS * HEAD_DIM), jnp.bfloat16)
    for micro_at in range(MB):
        grad_now = top_grad[micro_at]
        for section in reversed(range(SEGMENTS)):
            grad_now = layer_backward(saved_inputs[section, micro_at], scale_gains[section], out_proj[section], grad_now)
            result = result.at[section, micro_at].set(grad_now)
    return result
```

```python
import functools

import jax
import jax.numpy as jnp
from jax import lax
from jax.experimental import pallas as pl
from jax.experimental.pallas import tpu as pltpu
from jax.sharding import PartitionSpec as P

HEAD_DIM = 128
X_HEADS = 2
G_HEADS = 2
QUERY_SCALE = 1.0 / 12.0
SOFT_CAP = 50.0
MESH = pl.DeviceIdType.MESH
F32 = jnp.float32
BF16 = jnp.bfloat16
NT = (((1,), (1,)), ((), ()))


def cols(at, width):
    return pl.ds(pl.multiple_of(at * width, width), width)


def dot_nt(a, b):
    return lax.dot_general(a, b, NT, preferred_element_type=F32)


def dot_nn(a, b):
    return jnp.dot(a, b, preferred_element_type=F32)


def cascade_kernel(
    pair_count,
    x_hbm,
    gain_hbm,
    w_hbm,
    top_hbm,
    out_hbm,
    x_own,
    x_halo,
    gains,
    w_buf,
    g_buf,
    v_all,
    kg_all,
    qg_all,
    o_all,
    slopes,
    weight_t,
    hg_buf,
    acc,
    con_send,
    con_recv,
    gain_send_sem,
    gain_sem,
    w_send_sem,
    w_sem,
    top_sem,
    x_send_sem,
    x_sem,
    halo_send_sem,
    halo_sem,
    con_send_sem,
    con_sem,
    swap_send_sem,
    swap_sem,
    cross_send_sem,
    cross_sem,
    out_send_sem,
    out_sem,
):
    rows = x_hbm.shape[1]
    features = x_hbm.shape[2]
    half_width = features // 2
    heads = half_width // HEAD_DIM
    x_width = X_HEADS * HEAD_DIM
    g_width = G_HEADS * HEAD_DIM
    x_chunks = half_width // x_width
    g_chunks = half_width // g_width

    seg = lax.axis_index("segment")
    ctx = lax.axis_index("ctx")
    half = seg // 2
    core = seg % 2
    pair = ctx // 2
    side = ctx % 2
    upper = half == 1
    lower = half == 0
    mine = jnp.where(upper, side, 1 - side)
    held = 1 - core

    def place(half_at, core_at, pair_at, side_at):
        return (2 * half_at + core_at, 2 * pair_at + side_at)

    partner = place(half, 1 - core, pair, side)
    facing = place(1 - half, core, pair, 1 - side)
    later = place(half, core, lax.rem(pair + 1, pair_count), side)
    earlier = place(half, core, lax.rem(pair + pair_count - 1, pair_count), side)
    beside = place(half, core, pair, 1 - side)
    across = place(half, 1 - core, pair, 1 - side)

    def remote(src, dst, send_sem, recv_sem, device):
        return pltpu.make_async_remote_copy(
            src_ref=src,
            dst_ref=dst,
            send_sem=send_sem,
            recv_sem=recv_sem,
            device_id=device,
            device_id_type=MESH,
        )

    def gain_local():
        return pltpu.make_async_copy(
            gain_hbm.at[:, :, cols(core, half_width)], gains.at[held], gain_sem.at[held]
        )

    def gain_remote():
        return remote(
            gain_hbm.at[:, :, cols(1 - core, half_width)],
            gains.at[held],
            gain_send_sem,
            gain_sem.at[held],
            partner,
        )

    def gain_arrival(stage):
        return pltpu.make_async_copy(
            gain_hbm.at[:, :, cols(core, half_width)], gains.at[stage], gain_sem.at[stage]
        )

    def w_local():
        return pltpu.make_async_copy(
            w_hbm.at[cols(core, half_width), :], w_buf.at[held], w_sem.at[held]
        )

    def w_remote():
        return remote(
            w_hbm.at[cols(1 - core, half_width), :],
            w_buf.at[held],
            w_send_sem,
            w_sem.at[held],
            partner,
        )

    def w_arrival(stage):
        return pltpu.make_async_copy(
            w_hbm.at[cols(core, half_width), :], w_buf.at[stage], w_sem.at[stage]
        )

    def top_local():
        return pltpu.make_async_copy(
            top_hbm.at[mine], g_buf.at[0, cols(side, rows), :], top_sem
        )

    def x_local(i):
        return pltpu.make_async_copy(
            x_hbm.at[mine, :, cols(core * x_chunks + i, x_width)],
            x_own.at[held, cols(side, rows), cols(i, x_width)],
            x_sem.at[held, side, i],
        )

    def x_remote(i, way):
        micro = mine if way == 0 else 1 - mine
        core_at = core if way == 1 else 1 - core
        return remote(
            x_hbm.at[micro, :, cols(core_at * x_chunks + i, x_width)],
            x_own.at[held, cols(side, rows), cols(i, x_width)],
            x_send_sem.at[way, i],
            x_sem.at[held, side, i],
            (partner, beside, across)[way],
        )

    def x_arrival(stage, block, i):
        return pltpu.make_async_copy(
            x_hbm.at[mine, :, cols(core * x_chunks + i, x_width)],
            x_own.at[stage, cols(block, rows), cols(i, x_width)],
            x_sem.at[stage, block, i],
        )

    def halo_copy(stage, i):
        return remote(
            x_own.at[stage, :, cols(i, x_width)],
            x_halo.at[stage, :, cols(i, x_width)],
            halo_send_sem.at[stage, i],
            halo_sem.at[stage, i],
            later,
        )

    def con_copy(stage, h):
        return remote(
            con_send.at[stage, :, cols(h, HEAD_DIM)],
            con_recv.at[stage, :, cols(h, HEAD_DIM)],
            con_send_sem.at[stage, h],
            con_sem.at[stage, h],
            earlier,
        )

    def swap_copy(stage, f, core_at):
        ref = g_buf.at[stage, :, cols(core_at * g_chunks + f, g_width)]
        return remote(ref, ref, swap_send_sem.at[stage, f], swap_sem.at[stage, f], partner)

    def top_swap_copy(f, core_at):
        ref = g_buf.at[0, cols(1 - side, rows), cols(core_at * g_chunks + f, g_width)]
        return remote(ref, ref, swap_send_sem.at[0, f], swap_sem.at[0, f], partner)

    def down_copy(f):
        at = cols(core * g_chunks + f, g_width)
        return remote(
            g_buf.at[2, :, at], g_buf.at[0, :, at], cross_send_sem.at[f], cross_sem.at[f], facing
        )

    def top_copy(f, block):
        at = cols(core * g_chunks + f, g_width)
        return remote(
            top_hbm.at[mine, :, at],
            g_buf.at[0, cols(block, rows), at],
            cross_send_sem.at[f],
            cross_sem.at[f],
            facing,
        )

    def out_refs(stage, f, block):
        at = cols(core * g_chunks + f, g_width)
        return g_buf.at[stage + 1, cols(block, rows), at], out_hbm.at[mine, :, at]

    def out_local(stage, f):
        src, dst = out_refs(stage, f, side)
        return pltpu.make_async_copy(src, dst, out_sem.at[mine, core, f])

    def out_partner(stage, f):
        src, dst = out_refs(stage, f, side)
        return remote(
            src, dst, out_send_sem.at[stage, 0, f], out_sem.at[mine, core, f], partner
        )

    def out_beside(stage, f):
        src, dst = out_refs(stage, f, 1 - side)
        return remote(
            src,
            dst,
            out_send_sem.at[stage, 1, f],
            out_sem.at[mine, core, f],
            place(half, 1 - stage, pair, 1 - side),
        )

    def out_arrival(micro, core_at, f):
        at = cols(core_at * g_chunks + f, g_width)
        return pltpu.make_async_copy(
            g_buf.at[1, cols(0, rows), at], out_hbm.at[micro, :, at], out_sem.at[micro, core_at, f]
        )

    gain_local().start()
    for i in range(x_chunks):
        x_local(i).start()
    w_local().start()

    @pl.when(upper)
    def _():
        top_local().start()

    barrier = pltpu.get_barrier_semaphore()
    peers = (partner, facing, later, earlier, beside, across)
    for peer in peers:
        pl.semaphore_signal(barrier, inc=1, device_id=peer, device_id_type=MESH)
    pl.semaphore_wait(barrier, len(peers))

    def deliver():
        for i in range(x_chunks):
            for way in range(3):
                x_remote(i, way).start()

    @pl.when(core == 1)
    def _():
        deliver()

    gain_remote().start()

    @pl.when(lower)
    def _():
        for f in range(g_chunks):
            top_copy(f, side).start()

    w_remote().start()

    def forward(stage):
        for i in range(x_chunks):
            for block in range(2):
                x_arrival(stage, block, i).wait()
            halo_copy(stage, i).start()

    forward(0)

    @pl.when(core == 0)
    def _():
        deliver()

    for stage in range(2):
        gain_arrival(stage).wait()

    row_at = lax.broadcasted_iota(jnp.int32, (rows, rows), 0)
    col_at = lax.broadcasted_iota(jnp.int32, (rows, rows), 1)
    own = col_at <= row_at
    own_t = row_at <= col_at
    seen = (pair >= 1).astype(F32)

    def prepare_head(stage, h):
        at = cols(h, HEAD_DIM)
        gq, gk, gv = (gains[stage, n, :, at] for n in range(3))
        x = jnp.concatenate([x_halo[stage, :, at], x_own[stage, :, at]], axis=0).astype(F32)
        q = (x[2 * rows :] * gq).astype(BF16)
        k = (x * gk).astype(BF16)
        v = (x * gv).astype(BF16)
        v_all[stage, h] = v
        kg_all[stage, h] = (k.astype(F32) * gq).astype(BF16)
        qg_all[stage, h] = (q.astype(F32) * gk).astype(BF16)
        for block in range(2):
            low = block * rows
            span = slice(low, low + 3 * rows)
            s = dot_nt(q[low : low + rows], k[span]) * (QUERY_SCALE / SOFT_CAP)
            t_one = jnp.tanh(s[:, rows : 2 * rows])
            t_mix = jnp.tanh(jnp.where(own, s[:, 2 * rows :], s[:, :rows]))
            e_one = jnp.exp(SOFT_CAP * t_one)
            if block == 0:
                e_one = e_one * seen
            e_mix = jnp.exp(SOFT_CAP * t_mix)
            e_mix = jnp.where(own, e_mix, e_mix * seen)
            scale = 1.0 / jnp.sum(e_one + e_mix, axis=1, keepdims=True)
            w_one = e_one * scale
            w_mix = e_mix * scale
            slopes[stage, h, block, 0] = w_one * (1.0 - t_one * t_one) * QUERY_SCALE
            slopes[stage, h, block, 1] = w_mix * (1.0 - t_mix * t_mix) * QUERY_SCALE
            w_cat = jnp.concatenate(
                [jnp.where(own, 0.0, w_mix), w_one, jnp.where(own, w_mix, 0.0)], axis=1
            ).astype(BF16)
            o_all[stage, low : low + rows, at] = dot_nn(w_cat, v[span])
            wt_mix = w_mix.T
            weight_t[stage, h, block] = jnp.concatenate(
                [jnp.where(own_t, 0.0, wt_mix), w_one.T, jnp.where(own_t, wt_mix, 0.0)], axis=0
            ).astype(BF16)

    def attend_head(stage, h):
        at = cols(h, HEAD_DIM)
        gv = gains[stage, 2, :, at]
        both = []
        d_query = []
        for block in range(2):
            low = block * rows
            hg = hg_buf[low : low + rows, at]
            hg_f = hg.astype(F32)
            gw = dot_nt(hg, v_all[stage, h, low : low + 3 * rows])
            row_dot = jnp.sum(hg_f * o_all[stage, low : low + rows, at], axis=1, keepdims=True)
            d_one = slopes[stage, h, block, 0] * (gw[:, rows : 2 * rows] - row_dot)
            d_mix = slopes[stage, h, block, 1] * (
                jnp.where(own, gw[:, 2 * rows :], gw[:, :rows]) - row_dot
            )
            d_cat = jnp.concatenate(
                [jnp.where(own, 0.0, d_mix), d_one, jnp.where(own, d_mix, 0.0)], axis=1
            ).astype(BF16)
            dt_mix = d_mix.T
            d_t = jnp.concatenate(
                [jnp.where(own_t, 0.0, dt_mix), d_one.T, jnp.where(own_t, dt_mix, 0.0)], axis=0
            ).astype(BF16)
            left = jnp.concatenate([d_t, weight_t[stage, h, block]], axis=1)
            right = jnp.concatenate(
                [qg_all[stage, h, low : low + rows], (hg_f * gv).astype(BF16)], axis=0
            )
            both.append(dot_nn(left, right))
            d_query.append(dot_nn(d_cat, kg_all[stage, h, low : low + 3 * rows]))
        con_send[stage, :rows, at] = both[0][:rows].astype(BF16)
        con_send[stage, rows:, at] = (both[0][rows : 2 * rows] + both[1][:rows]).astype(BF16)
        g_at = cols(core * heads + h, HEAD_DIM)
        acc[:rows, at] = (
            g_buf[stage, :rows, g_at].astype(F32)
            + d_query[0]
            + both[0][2 * rows :]
            + both[1][rows : 2 * rows]
        )
        acc[rows:, at] = (
            g_buf[stage, rows:, g_at].astype(F32) + d_query[1] + both[1][2 * rows :]
        )

    def halo_wait(stage, h):
        @pl.when(h % X_HEADS == 0)
        def _():
            halo_copy(stage, h // X_HEADS).wait_recv()

    @pl.when(lower)
    def _():
        forward(1)

        def ahead(n, carry):
            halo_wait(n // heads, n % heads)
            prepare_head(n // heads, n % heads)
            return carry

        lax.fori_loop(0, 2 * heads, ahead, 0)

    def run_stage(stage, carry):
        @pl.when(stage == 0)
        def _():
            @pl.when(upper)
            def _():
                for f in range(g_chunks):
                    top_copy(f, 1 - side).wait_recv()
                    top_swap_copy(f, core).start()
                for f in range(g_chunks):
                    top_swap_copy(f, 1 - core).wait_recv()
                top_local().wait()

            @pl.when(lower)
            def _():
                for f in range(g_chunks):
                    down_copy(f).wait_recv()
                    swap_copy(0, f, core).start()
                for f in range(g_chunks):
                    swap_copy(0, f, 1 - core).wait_recv()

        @pl.when(stage == 1)
        def _():
            for f in range(g_chunks):
                swap_copy(1, f, 1 - core).wait_recv()

        w_arrival(stage).wait()

        def project(n, carry):
            at = cols(n, g_width)
            hg_buf[:, at] = dot_nt(g_buf[stage], w_buf[stage, at, :]).astype(BF16)
            return carry

        lax.fori_loop(0, g_chunks, project, 0)

        def attend(h, carry):
            @pl.when(upper)
            def _():
                halo_wait(stage, h)
                prepare_head(stage, h)

            attend_head(stage, h)
            con_copy(stage, h).start()

            @pl.when(upper & (stage == 0) & (h == heads // 2))
            def _():
                forward(1)

            return carry

        lax.fori_loop(0, heads, attend, 0)

        def finish(f, carry):
            for j in range(G_HEADS):
                con_copy(stage, f * G_HEADS + j).wait_recv()
            at = cols(f, g_width)
            total = acc[:, at] + con_recv[stage, :, at].astype(F32)
            g_buf[stage + 1, :, cols(core * g_chunks + f, g_width)] = total.astype(BF16)

            @pl.when(stage == 0)
            def _():
                swap_copy(1, f, core).start()

            @pl.when((stage == 1) & upper)
            def _():
                down_copy(f).start()

            @pl.when(core + stage == 1)
            def _():
                out_local(stage, f).start()

            @pl.when(core + stage != 1)
            def _():
                out_partner(stage, f).start()

            out_beside(stage, f).start()
            return carry

        lax.fori_loop(0, g_chunks, finish, 0)
        return carry

    lax.fori_loop(0, 2, run_stage, 0)

    gain_remote().wait_send()
    w_remote().wait_send()
    for i in range(x_chunks):
        for way in range(3):
            x_remote(i, way).wait_send()
        for stage in range(2):
            halo_copy(stage, i).wait_send()
    for f in range(g_chunks):
        swap_copy(1, f, core).wait_send()

        @pl.when(upper)
        def _():
            top_swap_copy(f, core).wait_send()
            down_copy(f).wait_send()

        @pl.when(lower)
        def _():
            swap_copy(0, f, core).wait_send()
            top_copy(f, side).wait_send()

        for stage in range(2):

            @pl.when(core + stage != 1)
            def _():
                out_partner(stage, f).wait_send()

            out_beside(stage, f).wait_send()
    for stage in range(2):
        for h in range(heads):
            con_copy(stage, h).wait_send()
    for micro in range(2):
        for core_at in range(2):
            for f in range(g_chunks):
                out_arrival(micro, core_at, f).wait()


def solution(mesh):
    pair_count = mesh.shape["ctx"] // 2

    def on_device(saved_inputs, scale_gains, out_proj, top_grad):
        _, micros, rows, features = saved_inputs.shape
        half_width = features // 2
        heads = half_width // HEAD_DIM
        x_chunks = heads // X_HEADS
        g_chunks = heads // G_HEADS
        dma = pltpu.SemaphoreType.DMA
        anywhere = pl.BlockSpec(memory_space=pl.ANY)
        result = pl.pallas_call(
            functools.partial(cascade_kernel, pair_count),
            out_shape=jax.ShapeDtypeStruct((micros, rows, features), BF16),
            in_specs=[anywhere] * 4,
            out_specs=anywhere,
            scratch_shapes=[
                pltpu.VMEM((2, 2 * rows, half_width), BF16),
                pltpu.VMEM((2, 2 * rows, half_width), BF16),
                pltpu.VMEM((2, 3, 1, half_width), F32),
                pltpu.VMEM((2, half_width, features), BF16),
                pltpu.VMEM((3, 2 * rows, features), BF16),
                pltpu.VMEM((2, heads, 4 * rows, HEAD_DIM), BF16),
                pltpu.VMEM((2, heads, 4 * rows, HEAD_DIM), BF16),
                pltpu.VMEM((2, heads, 2 * rows, HEAD_DIM), BF16),
                pltpu.VMEM((2, 2 * rows, half_width), F32),
                pltpu.VMEM((2, heads, 2, 2, rows, rows), F32),
                pltpu.VMEM((2, heads, 2, 3 * rows, rows), BF16),
                pltpu.VMEM((2 * rows, half_width), BF16),
                pltpu.VMEM((2 * rows, half_width), F32),
                pltpu.VMEM((2, 2 * rows, half_width), BF16),
                pltpu.VMEM((2, 2 * rows, half_width), BF16),
                dma,
                dma((2,)),
                dma,
                dma((2,)),
                dma,
                dma((3, x_chunks)),
                dma((2, 2, x_chunks)),
                dma((2, x_chunks)),
                dma((2, x_chunks)),
                dma((2, heads)),
                dma((2, heads)),
                dma((2, g_chunks)),
                dma((2, g_chunks)),
                dma((g_chunks,)),
                dma((g_chunks,)),
                dma((2, 2, g_chunks)),
                dma((2, 2, g_chunks)),
            ],
            compiler_params=pltpu.CompilerParams(collective_id=0, has_side_effects=True),
        )(saved_inputs[0], scale_gains.reshape(3, 1, features), out_proj[0], top_grad)
        return result[None]

    return jax.shard_map(
        on_device,
        mesh=mesh,
        in_specs=(
            P("segment", None, "ctx", None),
            P("segment", None, None),
            P("segment", None, None),
            P(None, "ctx", None),
        ),
        out_specs=P("segment", None, "ctx", None),
        check_vma=False,
    )
```

```python
import functools

import jax
import jax.numpy as jnp
from jax import lax
from jax.experimental import pallas as pl
from jax.experimental.pallas import tpu as pltpu
from jax.sharding import PartitionSpec as P

HEAD_DIM = 128
X_HEADS = 1
G_HEADS = 2
QUERY_SCALE = 1.0 / 12.0
SOFT_CAP = 50.0
MESH = pl.DeviceIdType.MESH
F32 = jnp.float32
BF16 = jnp.bfloat16
NT = (((1,), (1,)), ((), ()))


def cols(at, width):
    return pl.ds(pl.multiple_of(at * width, width), width)


def dot_nt(a, b):
    return lax.dot_general(a, b, NT, preferred_element_type=F32)


def dot_nn(a, b):
    return jnp.dot(a, b, preferred_element_type=F32)


def cascade_kernel(
    pair_count,
    x_hbm,
    gain_hbm,
    w_hbm,
    top_hbm,
    out_hbm,
    x_own,
    x_halo,
    gains,
    w_buf,
    g_buf,
    v_all,
    kg_all,
    qg_all,
    o_all,
    slopes,
    weight_t,
    hg_sum,
    acc,
    con_send,
    con_recv,
    gain_send_sem,
    gain_sem,
    w_send_sem,
    w_sem,
    top_sem,
    x_send_sem,
    x_sem,
    halo_send_sem,
    halo_sem,
    con_send_sem,
    con_sem,
    swap_send_sem,
    swap_sem,
    cross_send_sem,
    cross_sem,
    out_send_sem,
    out_sem,
):
    rows = x_hbm.shape[1]
    features = x_hbm.shape[2]
    half_width = features // 2
    heads = half_width // HEAD_DIM
    x_width = X_HEADS * HEAD_DIM
    g_width = G_HEADS * HEAD_DIM
    x_chunks = half_width // x_width
    g_chunks = half_width // g_width

    seg = lax.axis_index("segment")
    ctx = lax.axis_index("ctx")
    half = seg // 2
    core = seg % 2
    pair = ctx // 2
    side = ctx % 2
    upper = half == 1
    lower = half == 0
    mine = jnp.where(upper, side, 1 - side)
    held = 1 - core
    has_later = pair < pair_count - 1
    has_earlier = pair > 0

    def place(half_at, core_at, pair_at, side_at):
        return (2 * half_at + core_at, 2 * pair_at + side_at)

    partner = place(half, 1 - core, pair, side)
    facing = place(1 - half, core, pair, 1 - side)
    later = place(half, core, jnp.minimum(pair + 1, pair_count - 1), side)
    earlier = place(half, core, jnp.maximum(pair - 1, 0), side)
    beside = place(half, core, pair, 1 - side)
    across = place(half, 1 - core, pair, 1 - side)

    def remote(src, dst, send_sem, recv_sem, device):
        return pltpu.make_async_remote_copy(
            src_ref=src,
            dst_ref=dst,
            send_sem=send_sem,
            recv_sem=recv_sem,
            device_id=device,
            device_id_type=MESH,
        )

    def gain_local():
        return pltpu.make_async_copy(
            gain_hbm.at[:, :, cols(core, half_width)], gains.at[held], gain_sem.at[held]
        )

    def gain_remote():
        return remote(
            gain_hbm.at[:, :, cols(1 - core, half_width)],
            gains.at[held],
            gain_send_sem,
            gain_sem.at[held],
            partner,
        )

    def gain_arrival(stage):
        return pltpu.make_async_copy(
            gain_hbm.at[:, :, cols(core, half_width)], gains.at[stage], gain_sem.at[stage]
        )

    def w_local():
        return pltpu.make_async_copy(
            w_hbm.at[cols(core, half_width), :], w_buf.at[held], w_sem.at[held]
        )

    def w_remote():
        return remote(
            w_hbm.at[cols(1 - core, half_width), :],
            w_buf.at[held],
            w_send_sem,
            w_sem.at[held],
            partner,
        )

    def w_arrival(stage):
        return pltpu.make_async_copy(
            w_hbm.at[cols(core, half_width), :], w_buf.at[stage], w_sem.at[stage]
        )

    def top_local():
        return pltpu.make_async_copy(
            top_hbm.at[mine], g_buf.at[0, cols(side, rows), :], top_sem
        )

    def x_local(i):
        return pltpu.make_async_copy(
            x_hbm.at[mine, :, cols(core * x_chunks + i, x_width)],
            x_own.at[held, cols(side, rows), cols(i, x_width)],
            x_sem.at[held, side, i],
        )

    def x_remote(i, way):
        micro = mine if way == 0 else 1 - mine
        core_at = core if way == 1 else 1 - core
        return remote(
            x_hbm.at[micro, :, cols(core_at * x_chunks + i, x_width)],
            x_own.at[held, cols(side, rows), cols(i, x_width)],
            x_send_sem.at[way, i],
            x_sem.at[held, side, i],
            (partner, beside, across)[way],
        )

    def x_arrival(stage, block, i):
        return pltpu.make_async_copy(
            x_hbm.at[mine, :, cols(core * x_chunks + i, x_width)],
            x_own.at[stage, cols(block, rows), cols(i, x_width)],
            x_sem.at[stage, block, i],
        )

    def halo_copy(stage, i):
        return remote(
            x_own.at[stage, :, cols(i, x_width)],
            x_halo.at[stage, :, cols(i, x_width)],
            halo_send_sem.at[stage, i],
            halo_sem.at[stage, i],
            later,
        )

    def con_copy(stage, h):
        return remote(
            con_send.at[stage, :, cols(h, HEAD_DIM)],
            con_recv.at[stage, :, cols(h, HEAD_DIM)],
            con_send_sem.at[stage, h],
            con_sem.at[stage, h],
            earlier,
        )

    def swap_copy(stage, h, core_at):
        ref = g_buf.at[stage, :, cols(core_at * heads + h, HEAD_DIM)]
        return remote(ref, ref, swap_send_sem.at[stage, h], swap_sem.at[stage, h], partner)

    def top_swap_copy(h, core_at):
        ref = g_buf.at[0, cols(1 - side, rows), cols(core_at * heads + h, HEAD_DIM)]
        return remote(ref, ref, swap_send_sem.at[0, h], swap_sem.at[0, h], partner)

    def down_copy(h):
        at = cols(core * heads + h, HEAD_DIM)
        return remote(
            g_buf.at[2, :, at], g_buf.at[0, :, at], cross_send_sem.at[h], cross_sem.at[h], facing
        )

    def top_copy(h, block):
        at = cols(core * heads + h, HEAD_DIM)
        return remote(
            top_hbm.at[mine, :, at],
            g_buf.at[0, cols(block, rows), at],
            cross_send_sem.at[h],
            cross_sem.at[h],
            facing,
        )

    def out_refs(stage, f, block):
        at = cols(core * g_chunks + f, g_width)
        return g_buf.at[stage + 1, cols(block, rows), at], out_hbm.at[mine, :, at]

    def out_local(stage, f):
        src, dst = out_refs(stage, f, side)
        return pltpu.make_async_copy(src, dst, out_sem.at[mine, core, f])

    def out_partner(stage, f):
        src, dst = out_refs(stage, f, side)
        return remote(
            src, dst, out_send_sem.at[stage, 0, f], out_sem.at[mine, core, f], partner
        )

    def out_beside(stage, f):
        src, dst = out_refs(stage, f, 1 - side)
        return remote(
            src,
            dst,
            out_send_sem.at[stage, 1, f],
            out_sem.at[mine, core, f],
            place(half, 1 - stage, pair, 1 - side),
        )

    def out_arrival(micro, core_at, f):
        at = cols(core_at * g_chunks + f, g_width)
        return pltpu.make_async_copy(
            g_buf.at[1, cols(0, rows), at], out_hbm.at[micro, :, at], out_sem.at[micro, core_at, f]
        )

    gain_local().start()
    for i in range(x_chunks):
        x_local(i).start()
    w_local().start()

    @pl.when(upper)
    def _():
        top_local().start()

    barrier = pltpu.get_barrier_semaphore()
    for peer in (partner, facing, beside, across):
        pl.semaphore_signal(barrier, inc=1, device_id=peer, device_id_type=MESH)

    @pl.when(has_later)
    def _():
        pl.semaphore_signal(barrier, inc=1, device_id=later, device_id_type=MESH)

    @pl.when(has_earlier)
    def _():
        pl.semaphore_signal(barrier, inc=1, device_id=earlier, device_id_type=MESH)

    @pl.when(jnp.logical_not(has_earlier))
    def _():
        x_halo[...] = jnp.zeros_like(x_halo)

    @pl.when(jnp.logical_not(has_later))
    def _():
        con_recv[...] = jnp.zeros_like(con_recv)

    peers = 4 + has_later.astype(jnp.int32) + has_earlier.astype(jnp.int32)
    pl.semaphore_wait(barrier, peers)

    def deliver():
        for i in range(x_chunks):
            for way in range(3):
                x_remote(i, way).start()

    @pl.when(core == 1)
    def _():
        deliver()

    gain_remote().start()

    @pl.when(lower)
    def _():
        for h in range(heads):
            top_copy(h, side).start()

    w_remote().start()

    def forward(stage):
        for i in range(x_chunks):
            for block in range(2):
                x_arrival(stage, block, i).wait()

            @pl.when(has_later)
            def _():
                halo_copy(stage, i).start()

    forward(0)

    @pl.when(core == 0)
    def _():
        deliver()

    for stage in range(2):
        gain_arrival(stage).wait()

    row_at = lax.broadcasted_iota(jnp.int32, (rows, rows), 0)
    col_at = lax.broadcasted_iota(jnp.int32, (rows, rows), 1)
    own = col_at <= row_at
    own_t = row_at <= col_at
    seen = (pair >= 1).astype(F32)

    def prepare_head(stage, h):
        at = cols(h, HEAD_DIM)
        gq, gk, gv = (gains[stage, n, :, at] for n in range(3))
        x = jnp.concatenate([x_halo[stage, :, at], x_own[stage, :, at]], axis=0).astype(F32)
        q = (x[2 * rows :] * gq).astype(BF16)
        k = (x * gk).astype(BF16)
        v = (x * gv).astype(BF16)
        v_all[stage, h] = v
        kg_all[stage, h] = (k.astype(F32) * gq).astype(BF16)
        qg_all[stage, h] = (q.astype(F32) * gk).astype(BF16)
        for block in range(2):
            low = block * rows
            span = slice(low, low + 3 * rows)
            s = dot_nt(q[low : low + rows], k[span]) * (QUERY_SCALE / SOFT_CAP)
            t_one = jnp.tanh(s[:, rows : 2 * rows])
            t_mix = jnp.tanh(jnp.where(own, s[:, 2 * rows :], s[:, :rows]))
            e_one = jnp.exp(SOFT_CAP * t_one)
            if block == 0:
                e_one = e_one * seen
            e_mix = jnp.exp(SOFT_CAP * t_mix)
            e_mix = jnp.where(own, e_mix, e_mix * seen)
            scale = 1.0 / jnp.sum(e_one + e_mix, axis=1, keepdims=True)
            w_one = e_one * scale
            w_mix = e_mix * scale
            slopes[stage, h, block, 0] = w_one * (1.0 - t_one * t_one) * QUERY_SCALE
            slopes[stage, h, block, 1] = w_mix * (1.0 - t_mix * t_mix) * QUERY_SCALE
            w_cat = jnp.concatenate(
                [jnp.where(own, 0.0, w_mix), w_one, jnp.where(own, w_mix, 0.0)], axis=1
            ).astype(BF16)
            o_all[stage, low : low + rows, at] = dot_nn(w_cat, v[span])
            wt_mix = w_mix.T
            weight_t[stage, h, block] = jnp.concatenate(
                [jnp.where(own_t, 0.0, wt_mix), w_one.T, jnp.where(own_t, wt_mix, 0.0)], axis=0
            ).astype(BF16)

    def attend_head(stage, h):
        at = cols(h, HEAD_DIM)
        gv = gains[stage, 2, :, at]
        both = []
        d_query = []
        for block in range(2):
            low = block * rows
            hg = hg_sum[low : low + rows, at].astype(BF16)
            hg_f = hg.astype(F32)
            gw = dot_nt(hg, v_all[stage, h, low : low + 3 * rows])
            row_dot = jnp.sum(hg_f * o_all[stage, low : low + rows, at], axis=1, keepdims=True)
            d_one = slopes[stage, h, block, 0] * (gw[:, rows : 2 * rows] - row_dot)
            d_mix = slopes[stage, h, block, 1] * (
                jnp.where(own, gw[:, 2 * rows :], gw[:, :rows]) - row_dot
            )
            d_cat = jnp.concatenate(
                [jnp.where(own, 0.0, d_mix), d_one, jnp.where(own, d_mix, 0.0)], axis=1
            ).astype(BF16)
            dt_mix = d_mix.T
            d_t = jnp.concatenate(
                [jnp.where(own_t, 0.0, dt_mix), d_one.T, jnp.where(own_t, dt_mix, 0.0)], axis=0
            ).astype(BF16)
            left = jnp.concatenate([d_t, weight_t[stage, h, block]], axis=1)
            right = jnp.concatenate(
                [qg_all[stage, h, low : low + rows], (hg_f * gv).astype(BF16)], axis=0
            )
            both.append(dot_nn(left, right))
            d_query.append(dot_nn(d_cat, kg_all[stage, h, low : low + 3 * rows]))
        con_send[stage, :rows, at] = both[0][:rows].astype(BF16)
        con_send[stage, rows:, at] = (both[0][rows : 2 * rows] + both[1][:rows]).astype(BF16)
        g_at = cols(core * heads + h, HEAD_DIM)
        acc[:rows, at] = (
            g_buf[stage, :rows, g_at].astype(F32)
            + d_query[0]
            + both[0][2 * rows :]
            + both[1][rows : 2 * rows]
        )
        acc[rows:, at] = (
            g_buf[stage, rows:, g_at].astype(F32) + d_query[1] + both[1][2 * rows :]
        )

    def ready_head(stage, h):
        @pl.when(has_earlier)
        def _():
            halo_copy(stage, h).wait_recv()

        prepare_head(stage, h)

    def absorb(stage, k):
        at = cols(k, g_width)
        hg_sum[...] += dot_nt(g_buf[stage, :, at], w_buf[stage, :, at])

    def absorb_partner(stage, f):
        for j in range(G_HEADS):
            swap_copy(stage, f * G_HEADS + j, 1 - core).wait_recv()
        absorb(stage, (1 - core) * g_chunks + f)

    @pl.when(lower)
    def _():
        forward(1)

        def ahead(n, carry):
            ready_head(n // heads, n % heads)
            return carry

        lax.fori_loop(0, 2 * heads, ahead, 0)

    hg_sum[...] = jnp.zeros_like(hg_sum)
    w_arrival(0).wait()

    @pl.when(upper)
    def _():
        top_local().wait()
        for h in range(heads):
            top_copy(h, 1 - side).wait_recv()
            top_swap_copy(h, core).start()

        def take(f, carry):
            absorb(0, core * g_chunks + f)
            for j in range(G_HEADS):
                top_swap_copy(f * G_HEADS + j, 1 - core).wait_recv()
            absorb(0, (1 - core) * g_chunks + f)
            return carry

        lax.fori_loop(0, g_chunks, take, 0)
        ready_head(0, 0)

    @pl.when(lower)
    def _():
        def take(f, carry):
            @pl.when(f < g_chunks)
            def _():
                for j in range(G_HEADS):
                    down_copy(f * G_HEADS + j).wait_recv()
                    swap_copy(0, f * G_HEADS + j, core).start()
                absorb(0, core * g_chunks + f)

            @pl.when(f > 0)
            def _():
                absorb_partner(0, f - 1)

            return carry

        lax.fori_loop(0, g_chunks + 1, take, 0)

    def run_stage(stage, carry):
        def attend(h, carry):
            attend_head(stage, h)

            @pl.when(has_earlier)
            def _():
                con_copy(stage, h).start()

            @pl.when(upper & (stage == 0) & (h == 2))
            def _():
                forward(1)

            @pl.when(upper & (stage * heads + h < 2 * heads - 1))
            def _():
                ready_head(stage + (h + 1) // heads, (h + 1) % heads)

            return carry

        lax.fori_loop(0, heads, attend, 0)

        @pl.when(stage == 0)
        def _():
            hg_sum[...] = jnp.zeros_like(hg_sum)
            w_arrival(1).wait()

        def finish(f, carry):
            @pl.when(f < g_chunks)
            def _():
                for j in range(G_HEADS):
                    h = f * G_HEADS + j

                    @pl.when(has_later)
                    def _():
                        con_copy(stage, h).wait_recv()

                    at = cols(h, HEAD_DIM)
                    total = acc[:, at] + con_recv[stage, :, at].astype(F32)
                    g_buf[stage + 1, :, cols(core * heads + h, HEAD_DIM)] = total.astype(BF16)

                    @pl.when(stage == 0)
                    def _():
                        swap_copy(1, h, core).start()

                    @pl.when((stage == 1) & upper)
                    def _():
                        down_copy(h).start()

                out_beside(stage, f).start()

                @pl.when(core + stage == 1)
                def _():
                    out_local(stage, f).start()

                @pl.when(core + stage != 1)
                def _():
                    out_partner(stage, f).start()

                @pl.when(stage == 0)
                def _():
                    absorb(1, core * g_chunks + f)

            @pl.when((stage == 0) & (f > 0))
            def _():
                absorb_partner(1, f - 1)

            return carry

        lax.fori_loop(0, g_chunks + 1 - stage, finish, 0)
        return carry

    lax.fori_loop(0, 2, run_stage, 0)

    gain_remote().wait_send()
    w_remote().wait_send()
    for i in range(x_chunks):
        for way in range(3):
            x_remote(i, way).wait_send()

    @pl.when(has_later)
    def _():
        for stage in range(2):
            for i in range(x_chunks):
                halo_copy(stage, i).wait_send()

    @pl.when(has_earlier)
    def _():
        for stage in range(2):
            for h in range(heads):
                con_copy(stage, h).wait_send()

    for h in range(heads):
        swap_copy(1, h, core).wait_send()

    @pl.when(upper)
    def _():
        for h in range(heads):
            top_swap_copy(h, core).wait_send()
            down_copy(h).wait_send()

    @pl.when(lower)
    def _():
        for h in range(heads):
            swap_copy(0, h, core).wait_send()
            top_copy(h, side).wait_send()

    for stage in range(2):

        @pl.when(core + stage != 1)
        def _():
            for f in range(g_chunks):
                out_partner(stage, f).wait_send()

        for f in range(g_chunks):
            out_beside(stage, f).wait_send()

    for micro in range(2):
        for core_at in range(2):
            for f in range(g_chunks):
                out_arrival(micro, core_at, f).wait()


def solution(mesh):
    pair_count = mesh.shape["ctx"] // 2

    def on_device(saved_inputs, scale_gains, out_proj, top_grad):
        _, micros, rows, features = saved_inputs.shape
        half_width = features // 2
        heads = half_width // HEAD_DIM
        x_chunks = heads // X_HEADS
        g_chunks = heads // G_HEADS
        dma = pltpu.SemaphoreType.DMA
        anywhere = pl.BlockSpec(memory_space=pl.ANY)
        result = pl.pallas_call(
            functools.partial(cascade_kernel, pair_count),
            out_shape=jax.ShapeDtypeStruct((micros, rows, features), BF16),
            in_specs=[anywhere] * 4,
            out_specs=anywhere,
            scratch_shapes=[
                pltpu.VMEM((2, 2 * rows, half_width), BF16),
                pltpu.VMEM((2, 2 * rows, half_width), BF16),
                pltpu.VMEM((2, 3, 1, half_width), F32),
                pltpu.VMEM((2, half_width, features), BF16),
                pltpu.VMEM((3, 2 * rows, features), BF16),
                pltpu.VMEM((2, heads, 4 * rows, HEAD_DIM), BF16),
                pltpu.VMEM((2, heads, 4 * rows, HEAD_DIM), BF16),
                pltpu.VMEM((2, heads, 2 * rows, HEAD_DIM), BF16),
                pltpu.VMEM((2, 2 * rows, half_width), F32),
                pltpu.VMEM((2, heads, 2, 2, rows, rows), F32),
                pltpu.VMEM((2, heads, 2, 3 * rows, rows), BF16),
                pltpu.VMEM((2 * rows, half_width), F32),
                pltpu.VMEM((2 * rows, half_width), F32),
                pltpu.VMEM((2, 2 * rows, half_width), BF16),
                pltpu.VMEM((2, 2 * rows, half_width), BF16),
                dma,
                dma((2,)),
                dma,
                dma((2,)),
                dma,
                dma((3, x_chunks)),
                dma((2, 2, x_chunks)),
                dma((2, x_chunks)),
                dma((2, x_chunks)),
                dma((2, heads)),
                dma((2, heads)),
                dma((2, heads)),
                dma((2, heads)),
                dma((heads,)),
                dma((heads,)),
                dma((2, 2, g_chunks)),
                dma((2, 2, g_chunks)),
            ],
            compiler_params=pltpu.CompilerParams(collective_id=0, has_side_effects=True),
        )(saved_inputs[0], scale_gains.reshape(3, 1, features), out_proj[0], top_grad)
        return result[None]

    return jax.shard_map(
        on_device,
        mesh=mesh,
        in_specs=(
            P("segment", None, "ctx", None),
            P("segment", None, None),
            P("segment", None, None),
            P(None, "ctx", None),
        ),
        out_specs=P("segment", None, "ctx", None),
        check_vma=False,
    )
```

```python
import functools

import jax
import jax.numpy as jnp
from jax import lax
from jax.experimental import pallas as pl
from jax.experimental.pallas import tpu as pltpu
from jax.sharding import PartitionSpec as P

HEAD_DIM = 128
X_HEADS = 1
G_HEADS = 2
QUERY_SCALE = 1.0 / 12.0
SOFT_CAP = 50.0
MESH = pl.DeviceIdType.MESH
F32 = jnp.float32
BF16 = jnp.bfloat16
NT = (((1,), (1,)), ((), ()))


def cols(at, width):
    return pl.ds(pl.multiple_of(at * width, width), width)


def dot_nt(a, b):
    return lax.dot_general(a, b, NT, preferred_element_type=F32)


def dot_nn(a, b):
    return jnp.dot(a, b, preferred_element_type=F32)


def cascade_kernel(
    pair_count,
    x_hbm,
    gain_hbm,
    w_hbm,
    top_hbm,
    out_hbm,
    x_own,
    x_halo,
    gains,
    w_buf,
    g_buf,
    v_all,
    kg_all,
    qg_all,
    o_all,
    slopes,
    weight_t,
    hg_sum,
    acc,
    con_send,
    con_recv,
    gain_send_sem,
    gain_sem,
    w_send_sem,
    w_sem,
    top_sem,
    x_send_sem,
    x_sem,
    halo_send_sem,
    halo_sem,
    con_send_sem,
    con_sem,
    swap_send_sem,
    swap_sem,
    cross_send_sem,
    cross_sem,
    out_send_sem,
    out_sem,
):
    rows = x_hbm.shape[1]
    features = x_hbm.shape[2]
    half_width = features // 2
    heads = half_width // HEAD_DIM
    x_width = X_HEADS * HEAD_DIM
    g_width = G_HEADS * HEAD_DIM
    x_chunks = half_width // x_width
    g_chunks = half_width // g_width

    seg = lax.axis_index("segment")
    ctx = lax.axis_index("ctx")
    half = seg // 2
    core = seg % 2
    pair = ctx // 2
    side = ctx % 2
    upper = half == 1
    lower = half == 0
    mine = jnp.where(upper, side, 1 - side)
    held = 1 - core
    has_later = pair < pair_count - 1
    has_earlier = pair > 0

    def place(half_at, core_at, pair_at, side_at):
        return (2 * half_at + core_at, 2 * pair_at + side_at)

    partner = place(half, 1 - core, pair, side)
    facing = place(1 - half, core, pair, 1 - side)
    later = place(half, core, jnp.minimum(pair + 1, pair_count - 1), side)
    earlier = place(half, core, jnp.maximum(pair - 1, 0), side)
    beside = place(half, core, pair, 1 - side)
    across = place(half, 1 - core, pair, 1 - side)

    def remote(src, dst, send_sem, recv_sem, device):
        return pltpu.make_async_remote_copy(
            src_ref=src,
            dst_ref=dst,
            send_sem=send_sem,
            recv_sem=recv_sem,
            device_id=device,
            device_id_type=MESH,
        )

    def gain_local():
        return pltpu.make_async_copy(
            gain_hbm.at[:, :, cols(core, half_width)], gains.at[held], gain_sem.at[held]
        )

    def gain_remote():
        return remote(
            gain_hbm.at[:, :, cols(1 - core, half_width)],
            gains.at[held],
            gain_send_sem,
            gain_sem.at[held],
            partner,
        )

    def gain_arrival(stage):
        return pltpu.make_async_copy(
            gain_hbm.at[:, :, cols(core, half_width)], gains.at[stage], gain_sem.at[stage]
        )

    def w_local():
        return pltpu.make_async_copy(
            w_hbm.at[cols(core, half_width), :], w_buf.at[held], w_sem.at[held]
        )

    def w_remote():
        return remote(
            w_hbm.at[cols(1 - core, half_width), :],
            w_buf.at[held],
            w_send_sem,
            w_sem.at[held],
            partner,
        )

    def w_arrival(stage):
        return pltpu.make_async_copy(
            w_hbm.at[cols(core, half_width), :], w_buf.at[stage], w_sem.at[stage]
        )

    def top_local():
        return pltpu.make_async_copy(
            top_hbm.at[mine], g_buf.at[0, cols(side, rows), :], top_sem
        )

    def x_local(i):
        return pltpu.make_async_copy(
            x_hbm.at[mine, :, cols(core * x_chunks + i, x_width)],
            x_own.at[held, cols(side, rows), cols(i, x_width)],
            x_sem.at[held, side, i],
        )

    def x_remote(i, way):
        micro = mine if way == 0 else 1 - mine
        core_at = core if way == 1 else 1 - core
        return remote(
            x_hbm.at[micro, :, cols(core_at * x_chunks + i, x_width)],
            x_own.at[held, cols(side, rows), cols(i, x_width)],
            x_send_sem.at[way, i],
            x_sem.at[held, side, i],
            (partner, beside, across)[way],
        )

    def x_arrival(stage, block, i):
        return pltpu.make_async_copy(
            x_hbm.at[mine, :, cols(core * x_chunks + i, x_width)],
            x_own.at[stage, cols(block, rows), cols(i, x_width)],
            x_sem.at[stage, block, i],
        )

    def halo_copy(stage, i):
        return remote(
            x_own.at[stage, :, cols(i, x_width)],
            x_halo.at[stage, :, cols(i, x_width)],
            halo_send_sem.at[stage, i],
            halo_sem.at[stage, i],
            later,
        )

    def con_copy(stage, h):
        return remote(
            con_send.at[stage, :, cols(h, HEAD_DIM)],
            con_recv.at[stage, :, cols(h, HEAD_DIM)],
            con_send_sem.at[stage, h],
            con_sem.at[stage, h],
            earlier,
        )

    def swap_copy(stage, h, core_at):
        ref = g_buf.at[stage, :, cols(core_at * heads + h, HEAD_DIM)]
        return remote(ref, ref, swap_send_sem.at[stage, h], swap_sem.at[stage, h], partner)

    def top_swap_copy(h, core_at):
        ref = g_buf.at[0, cols(1 - side, rows), cols(core_at * heads + h, HEAD_DIM)]
        return remote(ref, ref, swap_send_sem.at[0, h], swap_sem.at[0, h], partner)

    def down_copy(h):
        at = cols(core * heads + h, HEAD_DIM)
        return remote(
            g_buf.at[2, :, at], g_buf.at[0, :, at], cross_send_sem.at[h], cross_sem.at[h], facing
        )

    def top_copy(h, block):
        at = cols(core * heads + h, HEAD_DIM)
        return remote(
            top_hbm.at[mine, :, at],
            g_buf.at[0, cols(block, rows), at],
            cross_send_sem.at[h],
            cross_sem.at[h],
            facing,
        )

    def out_refs(stage, h, block):
        at = cols(core * heads + h, HEAD_DIM)
        return g_buf.at[stage + 1, cols(block, rows), at], out_hbm.at[mine, :, at]

    def out_local(stage, h):
        src, dst = out_refs(stage, h, side)
        return pltpu.make_async_copy(src, dst, out_sem.at[mine, core, h])

    def out_partner(stage, h):
        src, dst = out_refs(stage, h, side)
        return remote(
            src, dst, out_send_sem.at[stage, 0, h], out_sem.at[mine, core, h], partner
        )

    def out_beside(stage, h):
        src, dst = out_refs(stage, h, 1 - side)
        return remote(
            src,
            dst,
            out_send_sem.at[stage, 1, h],
            out_sem.at[mine, core, h],
            place(half, 1 - stage, pair, 1 - side),
        )

    def out_arrival(micro, core_at, h):
        at = cols(core_at * heads + h, HEAD_DIM)
        return pltpu.make_async_copy(
            g_buf.at[1, cols(0, rows), at], out_hbm.at[micro, :, at], out_sem.at[micro, core_at, h]
        )

    gain_local().start()
    for i in range(x_chunks):
        x_local(i).start()
    w_local().start()

    @pl.when(upper)
    def _():
        top_local().start()

    barrier = pltpu.get_barrier_semaphore()
    for peer in (partner, facing, beside, across):
        pl.semaphore_signal(barrier, inc=1, device_id=peer, device_id_type=MESH)

    @pl.when(has_later)
    def _():
        pl.semaphore_signal(barrier, inc=1, device_id=later, device_id_type=MESH)

    @pl.when(has_earlier)
    def _():
        pl.semaphore_signal(barrier, inc=1, device_id=earlier, device_id_type=MESH)

    @pl.when(jnp.logical_not(has_earlier))
    def _():
        x_halo[...] = jnp.zeros_like(x_halo)

    @pl.when(jnp.logical_not(has_later))
    def _():
        con_recv[...] = jnp.zeros_like(con_recv)

    peers = 4 + has_later.astype(jnp.int32) + has_earlier.astype(jnp.int32)
    pl.semaphore_wait(barrier, peers)

    def deliver():
        for i in range(x_chunks):
            for way in range(3):
                x_remote(i, way).start()

    @pl.when(core == 1)
    def _():
        deliver()

    gain_remote().start()

    @pl.when(lower)
    def _():
        for h in range(heads):
            top_copy(h, side).start()

    w_remote().start()

    def forward(stage):
        for i in range(x_chunks):
            for block in range(2):
                x_arrival(stage, block, i).wait()

            @pl.when(has_later)
            def _():
                halo_copy(stage, i).start()

    forward(0)

    @pl.when(core == 0)
    def _():
        deliver()

    for stage in range(2):
        gain_arrival(stage).wait()

    row_at = lax.broadcasted_iota(jnp.int32, (rows, rows), 0)
    col_at = lax.broadcasted_iota(jnp.int32, (rows, rows), 1)
    own = col_at <= row_at
    own_t = row_at <= col_at
    seen = (pair >= 1).astype(F32)

    def prepare_head(stage, h):
        at = cols(h, HEAD_DIM)
        gq, gk, gv = (gains[stage, n, :, at] for n in range(3))
        x = jnp.concatenate([x_halo[stage, :, at], x_own[stage, :, at]], axis=0).astype(F32)
        q = (x[2 * rows :] * gq).astype(BF16)
        k = (x * gk).astype(BF16)
        v = (x * gv).astype(BF16)
        v_all[stage, h] = v
        kg_all[stage, h] = (k.astype(F32) * gq).astype(BF16)
        qg_all[stage, h] = (q.astype(F32) * gk).astype(BF16)
        for block in range(2):
            low = block * rows
            span = slice(low, low + 3 * rows)
            s = dot_nt(q[low : low + rows], k[span]) * (QUERY_SCALE / SOFT_CAP)
            t_one = jnp.tanh(s[:, rows : 2 * rows])
            t_mix = jnp.tanh(jnp.where(own, s[:, 2 * rows :], s[:, :rows]))
            e_one = jnp.exp(SOFT_CAP * t_one)
            if block == 0:
                e_one = e_one * seen
            e_mix = jnp.exp(SOFT_CAP * t_mix)
            e_mix = jnp.where(own, e_mix, e_mix * seen)
            scale = 1.0 / jnp.sum(e_one + e_mix, axis=1, keepdims=True)
            w_one = e_one * scale
            w_mix = e_mix * scale
            slopes[stage, h, block, 0] = w_one * (1.0 - t_one * t_one) * QUERY_SCALE
            slopes[stage, h, block, 1] = w_mix * (1.0 - t_mix * t_mix) * QUERY_SCALE
            w_cat = jnp.concatenate(
                [jnp.where(own, 0.0, w_mix), w_one, jnp.where(own, w_mix, 0.0)], axis=1
            ).astype(BF16)
            o_all[stage, low : low + rows, at] = dot_nn(w_cat, v[span])
            wt_mix = w_mix.T
            weight_t[stage, h, block] = jnp.concatenate(
                [jnp.where(own_t, 0.0, wt_mix), w_one.T, jnp.where(own_t, wt_mix, 0.0)], axis=0
            ).astype(BF16)

    def attend_head(stage, h):
        at = cols(h, HEAD_DIM)
        gv = gains[stage, 2, :, at]
        both = []
        d_query = []
        for block in range(2):
            low = block * rows
            hg = hg_sum[low : low + rows, at].astype(BF16)
            hg_f = hg.astype(F32)
            gw = dot_nt(hg, v_all[stage, h, low : low + 3 * rows])
            row_dot = jnp.sum(hg_f * o_all[stage, low : low + rows, at], axis=1, keepdims=True)
            d_one = slopes[stage, h, block, 0] * (gw[:, rows : 2 * rows] - row_dot)
            d_mix = slopes[stage, h, block, 1] * (
                jnp.where(own, gw[:, 2 * rows :], gw[:, :rows]) - row_dot
            )
            d_cat = jnp.concatenate(
                [jnp.where(own, 0.0, d_mix), d_one, jnp.where(own, d_mix, 0.0)], axis=1
            ).astype(BF16)
            d_t = d_cat.T
            left = jnp.concatenate([d_t, weight_t[stage, h, block]], axis=1)
            right = jnp.concatenate(
                [qg_all[stage, h, low : low + rows], (hg_f * gv).astype(BF16)], axis=0
            )
            both.append(dot_nn(left, right))
            d_query.append(dot_nn(d_cat, kg_all[stage, h, low : low + 3 * rows]))
        con_send[stage, :rows, at] = both[0][:rows].astype(BF16)
        con_send[stage, rows:, at] = (both[0][rows : 2 * rows] + both[1][:rows]).astype(BF16)
        g_at = cols(core * heads + h, HEAD_DIM)
        acc[:rows, at] = (
            g_buf[stage, :rows, g_at].astype(F32)
            + d_query[0]
            + both[0][2 * rows :]
            + both[1][rows : 2 * rows]
        )
        acc[rows:, at] = (
            g_buf[stage, rows:, g_at].astype(F32) + d_query[1] + both[1][2 * rows :]
        )

    def ready_head(stage, h):
        @pl.when(has_earlier)
        def _():
            halo_copy(stage, h).wait_recv()

        prepare_head(stage, h)

    def absorb(stage, k):
        at = cols(k, g_width)
        hg_sum[...] += dot_nt(g_buf[stage, :, at], w_buf[stage, :, at])

    def absorb_partner(stage, f):
        for j in range(G_HEADS):
            swap_copy(stage, f * G_HEADS + j, 1 - core).wait_recv()
        absorb(stage, (1 - core) * g_chunks + f)

    @pl.when(lower)
    def _():
        forward(1)

        def ahead(n, carry):
            ready_head(n // heads, n % heads)
            return carry

        lax.fori_loop(0, 2 * heads, ahead, 0)

    hg_sum[...] = jnp.zeros_like(hg_sum)
    w_arrival(0).wait()

    @pl.when(upper)
    def _():
        top_local().wait()
        for h in range(heads):
            top_copy(h, 1 - side).wait_recv()
            top_swap_copy(h, core).start()

        def take(f, carry):
            absorb(0, core * g_chunks + f)
            for j in range(G_HEADS):
                top_swap_copy(f * G_HEADS + j, 1 - core).wait_recv()
            absorb(0, (1 - core) * g_chunks + f)
            return carry

        lax.fori_loop(0, g_chunks, take, 0)
        ready_head(0, 0)

    @pl.when(lower)
    def _():
        def take(f, carry):
            @pl.when(f < g_chunks)
            def _():
                for j in range(G_HEADS):
                    down_copy(f * G_HEADS + j).wait_recv()
                    swap_copy(0, f * G_HEADS + j, core).start()
                absorb(0, core * g_chunks + f)

            @pl.when(f > 0)
            def _():
                absorb_partner(0, f - 1)

            return carry

        lax.fori_loop(0, g_chunks + 1, take, 0)

    def run_stage(stage, carry):
        def send(h):
            @pl.when(has_earlier)
            def _():
                con_copy(stage, h).start()

        def attend(h, carry):
            attend_head(stage, h)
            send(h)
            return carry

        def attend_ahead(h, carry):
            @pl.when(has_earlier)
            def _():
                halo_copy(stage, h + 1).wait_recv()

            attend_head(stage, h)
            prepare_head(stage, h + 1)
            send(h)

            @pl.when((stage == 0) & (h == 2))
            def _():
                forward(1)

            return carry

        @pl.when(upper)
        def _():
            lax.fori_loop(0, heads - 1, attend_ahead, 0)

        lax.fori_loop(jnp.where(upper, heads - 1, 0), heads, attend, 0)

        @pl.when(upper & (stage == 0))
        def _():
            ready_head(1, 0)

        @pl.when(stage == 0)
        def _():
            hg_sum[...] = jnp.zeros_like(hg_sum)
            w_arrival(1).wait()

        def finish(f, carry):
            @pl.when(f < g_chunks)
            def _():
                for j in range(G_HEADS):
                    h = f * G_HEADS + j

                    @pl.when(has_later)
                    def _():
                        con_copy(stage, h).wait_recv()

                    at = cols(h, HEAD_DIM)
                    total = acc[:, at] + con_recv[stage, :, at].astype(F32)
                    g_buf[stage + 1, :, cols(core * heads + h, HEAD_DIM)] = total.astype(BF16)

                    @pl.when(stage == 0)
                    def _():
                        swap_copy(1, h, core).start()

                    @pl.when((stage == 1) & upper)
                    def _():
                        down_copy(h).start()

                    out_beside(stage, h).start()

                    @pl.when(core + stage == 1)
                    def _():
                        out_local(stage, h).start()

                    @pl.when(core + stage != 1)
                    def _():
                        out_partner(stage, h).start()

                @pl.when(stage == 0)
                def _():
                    absorb(1, core * g_chunks + f)

            @pl.when((stage == 0) & (f > 0))
            def _():
                absorb_partner(1, f - 1)

            return carry

        lax.fori_loop(0, g_chunks + 1 - stage, finish, 0)
        return carry

    lax.fori_loop(0, 2, run_stage, 0)

    gain_remote().wait_send()
    w_remote().wait_send()
    for i in range(x_chunks):
        for way in range(3):
            x_remote(i, way).wait_send()

    @pl.when(has_later)
    def _():
        for stage in range(2):
            for i in range(x_chunks):
                halo_copy(stage, i).wait_send()

    @pl.when(has_earlier)
    def _():
        for stage in range(2):
            for h in range(heads):
                con_copy(stage, h).wait_send()

    for h in range(heads):
        swap_copy(1, h, core).wait_send()

    @pl.when(upper)
    def _():
        for h in range(heads):
            top_swap_copy(h, core).wait_send()
            down_copy(h).wait_send()

    @pl.when(lower)
    def _():
        for h in range(heads):
            swap_copy(0, h, core).wait_send()
            top_copy(h, side).wait_send()

    for stage in range(2):

        @pl.when(core + stage != 1)
        def _():
            for h in range(heads):
                out_partner(stage, h).wait_send()

        for h in range(heads):
            out_beside(stage, h).wait_send()

    for micro in range(2):
        for core_at in range(2):
            for h in range(heads):
                out_arrival(micro, core_at, h).wait()


def solution(mesh):
    pair_count = mesh.shape["ctx"] // 2

    def on_device(saved_inputs, scale_gains, out_proj, top_grad):
        _, micros, rows, features = saved_inputs.shape
        half_width = features // 2
        heads = half_width // HEAD_DIM
        x_chunks = heads // X_HEADS
        g_chunks = heads // G_HEADS
        dma = pltpu.SemaphoreType.DMA
        anywhere = pl.BlockSpec(memory_space=pl.ANY)
        result = pl.pallas_call(
            functools.partial(cascade_kernel, pair_count),
            out_shape=jax.ShapeDtypeStruct((micros, rows, features), BF16),
            in_specs=[anywhere] * 4,
            out_specs=anywhere,
            scratch_shapes=[
                pltpu.VMEM((2, 2 * rows, half_width), BF16),
                pltpu.VMEM((2, 2 * rows, half_width), BF16),
                pltpu.VMEM((2, 3, 1, half_width), F32),
                pltpu.VMEM((2, half_width, features), BF16),
                pltpu.VMEM((3, 2 * rows, features), BF16),
                pltpu.VMEM((2, heads, 4 * rows, HEAD_DIM), BF16),
                pltpu.VMEM((2, heads, 4 * rows, HEAD_DIM), BF16),
                pltpu.VMEM((2, heads, 2 * rows, HEAD_DIM), BF16),
                pltpu.VMEM((2, 2 * rows, half_width), F32),
                pltpu.VMEM((2, heads, 2, 2, rows, rows), F32),
                pltpu.VMEM((2, heads, 2, 3 * rows, rows), BF16),
                pltpu.VMEM((2 * rows, half_width), F32),
                pltpu.VMEM((2 * rows, half_width), F32),
                pltpu.VMEM((2, 2 * rows, half_width), BF16),
                pltpu.VMEM((2, 2 * rows, half_width), BF16),
                dma,
                dma((2,)),
                dma,
                dma((2,)),
                dma,
                dma((3, x_chunks)),
                dma((2, 2, x_chunks)),
                dma((2, x_chunks)),
                dma((2, x_chunks)),
                dma((2, heads)),
                dma((2, heads)),
                dma((2, heads)),
                dma((2, heads)),
                dma((heads,)),
                dma((heads,)),
                dma((2, 2, heads)),
                dma((2, 2, heads)),
            ],
            compiler_params=pltpu.CompilerParams(collective_id=0, has_side_effects=True),
        )(saved_inputs[0], scale_gains.reshape(3, 1, features), out_proj[0], top_grad)
        return result[None]

    return jax.shard_map(
        on_device,
        mesh=mesh,
        in_specs=(
            P("segment", None, "ctx", None),
            P("segment", None, None),
            P("segment", None, None),
            P(None, "ctx", None),
        ),
        out_specs=P("segment", None, "ctx", None),
        check_vma=False,
    )
```

```python
import functools

import jax
import jax.numpy as jnp
from jax import lax
from jax.experimental import pallas as pl
from jax.experimental.pallas import tpu as pltpu
from jax.sharding import PartitionSpec as P

HEAD_DIM = 128
X_HEADS = 1
G_HEADS = 2
QUERY_SCALE = 1.0 / 12.0
SOFT_CAP = 50.0
MESH = pl.DeviceIdType.MESH
F32 = jnp.float32
BF16 = jnp.bfloat16
NT = (((1,), (1,)), ((), ()))


def cols(at, width):
    return pl.ds(pl.multiple_of(at * width, width), width)


def dot_nt(a, b):
    return lax.dot_general(a, b, NT, preferred_element_type=F32)


def dot_nn(a, b):
    return jnp.dot(a, b, preferred_element_type=F32)


def cascade_kernel(
    pair_count,
    x_hbm,
    gain_hbm,
    w_hbm,
    top_hbm,
    out_hbm,
    x_own,
    x_halo,
    gains,
    w_buf,
    g_buf,
    v_all,
    kg_all,
    qg_all,
    o_all,
    slopes,
    weight_t,
    hg_sum,
    acc,
    con_send,
    con_recv,
    gain_send_sem,
    gain_sem,
    w_send_sem,
    w_sem,
    top_sem,
    x_send_sem,
    x_sem,
    halo_send_sem,
    halo_sem,
    con_send_sem,
    con_sem,
    swap_send_sem,
    swap_sem,
    cross_send_sem,
    cross_sem,
    out_send_sem,
    out_sem,
):
    rows = x_hbm.shape[1]
    features = x_hbm.shape[2]
    half_width = features // 2
    heads = half_width // HEAD_DIM
    x_width = X_HEADS * HEAD_DIM
    g_width = G_HEADS * HEAD_DIM
    x_chunks = half_width // x_width
    g_chunks = half_width // g_width

    seg = lax.axis_index("segment")
    ctx = lax.axis_index("ctx")
    half = seg // 2
    core = seg % 2
    pair = ctx // 2
    side = ctx % 2
    upper = half == 1
    lower = half == 0
    mine = jnp.where(upper, side, 1 - side)
    held = 1 - core
    has_later = pair < pair_count - 1
    has_earlier = pair > 0

    def place(half_at, core_at, pair_at, side_at):
        return (2 * half_at + core_at, 2 * pair_at + side_at)

    partner = place(half, 1 - core, pair, side)
    facing = place(1 - half, core, pair, 1 - side)
    later = place(half, core, jnp.minimum(pair + 1, pair_count - 1), side)
    earlier = place(half, core, jnp.maximum(pair - 1, 0), side)
    beside = place(half, core, pair, 1 - side)
    across = place(half, 1 - core, pair, 1 - side)

    def remote(src, dst, send_sem, recv_sem, device):
        return pltpu.make_async_remote_copy(
            src_ref=src,
            dst_ref=dst,
            send_sem=send_sem,
            recv_sem=recv_sem,
            device_id=device,
            device_id_type=MESH,
        )

    def gain_local():
        return pltpu.make_async_copy(
            gain_hbm.at[:, :, cols(core, half_width)], gains.at[held], gain_sem.at[held]
        )

    def gain_remote():
        return remote(
            gain_hbm.at[:, :, cols(1 - core, half_width)],
            gains.at[held],
            gain_send_sem,
            gain_sem.at[held],
            partner,
        )

    def gain_arrival(stage):
        return pltpu.make_async_copy(
            gain_hbm.at[:, :, cols(core, half_width)], gains.at[stage], gain_sem.at[stage]
        )

    def w_local():
        return pltpu.make_async_copy(
            w_hbm.at[cols(core, half_width), :], w_buf.at[held], w_sem.at[held]
        )

    def w_remote():
        return remote(
            w_hbm.at[cols(1 - core, half_width), :],
            w_buf.at[held],
            w_send_sem,
            w_sem.at[held],
            partner,
        )

    def w_arrival(stage):
        return pltpu.make_async_copy(
            w_hbm.at[cols(core, half_width), :], w_buf.at[stage], w_sem.at[stage]
        )

    def top_local():
        return pltpu.make_async_copy(
            top_hbm.at[mine], g_buf.at[0, cols(side, rows), :], top_sem
        )

    def x_local(i):
        return pltpu.make_async_copy(
            x_hbm.at[mine, :, cols(core * x_chunks + i, x_width)],
            x_own.at[held, cols(side, rows), cols(i, x_width)],
            x_sem.at[held, side, i],
        )

    def x_remote(i, way):
        micro = mine if way == 0 else 1 - mine
        core_at = core if way == 1 else 1 - core
        return remote(
            x_hbm.at[micro, :, cols(core_at * x_chunks + i, x_width)],
            x_own.at[held, cols(side, rows), cols(i, x_width)],
            x_send_sem.at[way, i],
            x_sem.at[held, side, i],
            (partner, beside, across)[way],
        )

    def x_arrival(stage, block, i):
        return pltpu.make_async_copy(
            x_hbm.at[mine, :, cols(core * x_chunks + i, x_width)],
            x_own.at[stage, cols(block, rows), cols(i, x_width)],
            x_sem.at[stage, block, i],
        )

    def halo_copy(stage, i):
        return remote(
            x_own.at[stage, :, cols(i, x_width)],
            x_halo.at[stage, :, cols(i, x_width)],
            halo_send_sem.at[stage, i],
            halo_sem.at[stage, i],
            later,
        )

    def con_copy(stage, h):
        return remote(
            con_send.at[stage, :, cols(h, HEAD_DIM)],
            con_recv.at[stage, :, cols(h, HEAD_DIM)],
            con_send_sem.at[stage, h],
            con_sem.at[stage, h],
            earlier,
        )

    def swap_copy(stage, h, core_at):
        ref = g_buf.at[stage, :, cols(core_at * heads + h, HEAD_DIM)]
        return remote(ref, ref, swap_send_sem.at[stage, h], swap_sem.at[stage, h], partner)

    def top_swap_copy(h, core_at):
        ref = g_buf.at[0, cols(1 - side, rows), cols(core_at * heads + h, HEAD_DIM)]
        return remote(ref, ref, swap_send_sem.at[0, h], swap_sem.at[0, h], partner)

    def down_copy(h):
        at = cols(core * heads + h, HEAD_DIM)
        return remote(
            g_buf.at[2, :, at], g_buf.at[0, :, at], cross_send_sem.at[h], cross_sem.at[h], facing
        )

    def top_copy(h, block):
        at = cols(core * heads + h, HEAD_DIM)
        return remote(
            top_hbm.at[mine, :, at],
            g_buf.at[0, cols(block, rows), at],
            cross_send_sem.at[h],
            cross_sem.at[h],
            facing,
        )

    def out_refs(stage, h, block):
        at = cols(core * heads + h, HEAD_DIM)
        return g_buf.at[stage + 1, cols(block, rows), at], out_hbm.at[mine, :, at]

    def out_local(stage, h):
        src, dst = out_refs(stage, h, side)
        return pltpu.make_async_copy(src, dst, out_sem.at[mine, core, h])

    def out_partner(stage, h):
        src, dst = out_refs(stage, h, side)
        return remote(
            src, dst, out_send_sem.at[stage, 0, h], out_sem.at[mine, core, h], partner
        )

    def out_beside(stage, h):
        src, dst = out_refs(stage, h, 1 - side)
        return remote(
            src,
            dst,
            out_send_sem.at[stage, 1, h],
            out_sem.at[mine, core, h],
            place(half, 1 - stage, pair, 1 - side),
        )

    def out_arrival(micro, core_at, h):
        at = cols(core_at * heads + h, HEAD_DIM)
        return pltpu.make_async_copy(
            g_buf.at[1, cols(0, rows), at], out_hbm.at[micro, :, at], out_sem.at[micro, core_at, h]
        )

    gain_local().start()
    for i in range(x_chunks):
        x_local(i).start()
    w_local().start()

    @pl.when(upper)
    def _():
        top_local().start()

    barrier = pltpu.get_barrier_semaphore()
    for peer in (partner, facing, beside, across):
        pl.semaphore_signal(barrier, inc=1, device_id=peer, device_id_type=MESH)

    @pl.when(has_later)
    def _():
        pl.semaphore_signal(barrier, inc=1, device_id=later, device_id_type=MESH)

    @pl.when(has_earlier)
    def _():
        pl.semaphore_signal(barrier, inc=1, device_id=earlier, device_id_type=MESH)

    @pl.when(jnp.logical_not(has_earlier))
    def _():
        x_halo[...] = jnp.zeros_like(x_halo)

    @pl.when(jnp.logical_not(has_later))
    def _():
        con_recv[...] = jnp.zeros_like(con_recv)

    peers = 4 + has_later.astype(jnp.int32) + has_earlier.astype(jnp.int32)
    pl.semaphore_wait(barrier, peers)

    def deliver():
        for i in range(x_chunks):
            for way in range(3):
                x_remote(i, way).start()

    @pl.when(core == 1)
    def _():
        deliver()

    gain_remote().start()

    @pl.when(lower)
    def _():
        for h in range(heads):
            top_copy(h, side).start()

    w_remote().start()

    def forward_one(stage, i):
        for block in range(2):
            x_arrival(stage, block, i).wait()

        @pl.when(has_later)
        def _():
            halo_copy(stage, i).start()

    def forward(stage):
        for i in range(x_chunks):
            forward_one(stage, i)

    forward(0)

    @pl.when(core == 0)
    def _():
        deliver()

    for stage in range(2):
        gain_arrival(stage).wait()

    row_at = lax.broadcasted_iota(jnp.int32, (rows, rows), 0)
    col_at = lax.broadcasted_iota(jnp.int32, (rows, rows), 1)
    own = col_at <= row_at
    own_t = row_at <= col_at
    seen = (pair >= 1).astype(F32)

    def prepare_head(stage, h):
        at = cols(h, HEAD_DIM)
        gq, gk, gv = (gains[stage, n, :, at] for n in range(3))
        x = jnp.concatenate([x_halo[stage, :, at], x_own[stage, :, at]], axis=0).astype(F32)
        q = (x[2 * rows :] * gq).astype(BF16)
        k = (x * gk).astype(BF16)
        v = (x * gv).astype(BF16)
        v_all[stage, h] = v
        kg_all[stage, h] = (k.astype(F32) * gq).astype(BF16)
        qg_all[stage, h] = (q.astype(F32) * gk).astype(BF16)
        for block in range(2):
            low = block * rows
            span = slice(low, low + 3 * rows)
            s = dot_nt(q[low : low + rows], k[span]) * (QUERY_SCALE / SOFT_CAP)
            t_one = jnp.tanh(s[:, rows : 2 * rows])
            t_mix = jnp.tanh(jnp.where(own, s[:, 2 * rows :], s[:, :rows]))
            e_one = jnp.exp(SOFT_CAP * t_one)
            if block == 0:
                e_one = e_one * seen
            e_mix = jnp.exp(SOFT_CAP * t_mix)
            e_mix = jnp.where(own, e_mix, e_mix * seen)
            scale = 1.0 / jnp.sum(e_one + e_mix, axis=1, keepdims=True)
            w_one = e_one * scale
            w_mix = e_mix * scale
            slopes[stage, h, block, 0] = w_one * (1.0 - t_one * t_one) * QUERY_SCALE
            slopes[stage, h, block, 1] = w_mix * (1.0 - t_mix * t_mix) * QUERY_SCALE
            w_cat = jnp.concatenate(
                [jnp.where(own, 0.0, w_mix), w_one, jnp.where(own, w_mix, 0.0)], axis=1
            ).astype(BF16)
            o_all[stage, low : low + rows, at] = dot_nn(w_cat, v[span])
            wt_mix = w_mix.T
            weight_t[stage, h, block] = jnp.concatenate(
                [jnp.where(own_t, 0.0, wt_mix), w_one.T, jnp.where(own_t, wt_mix, 0.0)], axis=0
            ).astype(BF16)

    def attend_head(stage, h):
        at = cols(h, HEAD_DIM)
        gv = gains[stage, 2, :, at]
        both = []
        d_query = []
        for block in range(2):
            low = block * rows
            hg = hg_sum[low : low + rows, at].astype(BF16)
            hg_f = hg.astype(F32)
            gw = dot_nt(hg, v_all[stage, h, low : low + 3 * rows])
            row_dot = jnp.sum(hg_f * o_all[stage, low : low + rows, at], axis=1, keepdims=True)
            d_one = slopes[stage, h, block, 0] * (gw[:, rows : 2 * rows] - row_dot)
            d_mix = slopes[stage, h, block, 1] * (
                jnp.where(own, gw[:, 2 * rows :], gw[:, :rows]) - row_dot
            )
            d_cat = jnp.concatenate(
                [jnp.where(own, 0.0, d_mix), d_one, jnp.where(own, d_mix, 0.0)], axis=1
            ).astype(BF16)
            d_t = d_cat.T
            left = jnp.concatenate([d_t, weight_t[stage, h, block]], axis=1)
            right = jnp.concatenate(
                [qg_all[stage, h, low : low + rows], (hg_f * gv).astype(BF16)], axis=0
            )
            both.append(dot_nn(left, right))
            d_query.append(dot_nn(d_cat, kg_all[stage, h, low : low + 3 * rows]))
        con_send[stage, :rows, at] = both[0][:rows].astype(BF16)
        con_send[stage, rows:, at] = (both[0][rows : 2 * rows] + both[1][:rows]).astype(BF16)
        g_at = cols(core * heads + h, HEAD_DIM)
        acc[:rows, at] = (
            g_buf[stage, :rows, g_at].astype(F32)
            + d_query[0]
            + both[0][2 * rows :]
            + both[1][rows : 2 * rows]
        )
        acc[rows:, at] = (
            g_buf[stage, rows:, g_at].astype(F32) + d_query[1] + both[1][2 * rows :]
        )

    def ready_head(stage, h):
        @pl.when(has_earlier)
        def _():
            halo_copy(stage, h).wait_recv()

        prepare_head(stage, h)

    def absorb(stage, k):
        at = cols(k, g_width)
        hg_sum[...] += dot_nt(g_buf[stage, :, at], w_buf[stage, :, at])

    def absorb_partner(stage, f):
        for j in range(G_HEADS):
            swap_copy(stage, f * G_HEADS + j, 1 - core).wait_recv()
        absorb(stage, (1 - core) * g_chunks + f)

    @pl.when(lower)
    def _():
        forward(1)

        def ahead(n, carry):
            ready_head(n // heads, n % heads)
            return carry

        lax.fori_loop(0, 2 * heads, ahead, 0)

    hg_sum[...] = jnp.zeros_like(hg_sum)
    w_arrival(0).wait()

    @pl.when(upper)
    def _():
        top_local().wait()
        for h in range(heads):
            top_copy(h, 1 - side).wait_recv()
            top_swap_copy(h, core).start()

        def take(f, carry):
            absorb(0, core * g_chunks + f)
            for j in range(G_HEADS):
                top_swap_copy(f * G_HEADS + j, 1 - core).wait_recv()
            absorb(0, (1 - core) * g_chunks + f)
            return carry

        lax.fori_loop(0, g_chunks, take, 0)
        ready_head(0, 0)

    @pl.when(lower)
    def _():
        def take(f, carry):
            @pl.when(f < g_chunks)
            def _():
                for j in range(G_HEADS):
                    down_copy(f * G_HEADS + j).wait_recv()
                    swap_copy(0, f * G_HEADS + j, core).start()
                absorb(0, core * g_chunks + f)

            @pl.when(f > 0)
            def _():
                absorb_partner(0, f - 1)

            return carry

        lax.fori_loop(0, g_chunks + 1, take, 0)

    def run_stage(stage, carry):
        def send(h):
            @pl.when(has_earlier)
            def _():
                con_copy(stage, h).start()

        def attend(h, carry):
            attend_head(stage, h)
            send(h)
            return carry

        def attend_ahead(h, carry):
            @pl.when(has_earlier)
            def _():
                halo_copy(stage, h + 1).wait_recv()

            attend_head(stage, h)
            prepare_head(stage, h + 1)
            send(h)

            @pl.when((stage == 0) & (h >= 0))
            def _():
                forward_one(1, h - 0)

            @pl.when((stage == 0) & (h == heads - 2))
            def _():
                for i in range(x_chunks - 1, x_chunks):
                    forward_one(1, i)

            return carry

        @pl.when(upper)
        def _():
            lax.fori_loop(0, heads - 1, attend_ahead, 0)

        lax.fori_loop(jnp.where(upper, heads - 1, 0), heads, attend, 0)

        @pl.when(upper & (stage == 0))
        def _():
            ready_head(1, 0)

        @pl.when(stage == 0)
        def _():
            hg_sum[...] = jnp.zeros_like(hg_sum)
            w_arrival(1).wait()

        def finish(f, carry):
            @pl.when(f < g_chunks)
            def _():
                for j in range(G_HEADS):
                    h = f * G_HEADS + j

                    @pl.when(has_later)
                    def _():
                        con_copy(stage, h).wait_recv()

                    at = cols(h, HEAD_DIM)
                    total = acc[:, at] + con_recv[stage, :, at].astype(F32)
                    g_buf[stage + 1, :, cols(core * heads + h, HEAD_DIM)] = total.astype(BF16)

                    @pl.when(stage == 0)
                    def _():
                        swap_copy(1, h, core).start()

                    @pl.when((stage == 1) & upper)
                    def _():
                        down_copy(h).start()

                    out_beside(stage, h).start()

                    @pl.when(core + stage == 1)
                    def _():
                        out_local(stage, h).start()

                    @pl.when(core + stage != 1)
                    def _():
                        out_partner(stage, h).start()

                @pl.when(stage == 0)
                def _():
                    absorb(1, core * g_chunks + f)

            @pl.when((stage == 0) & (f > 0))
            def _():
                absorb_partner(1, f - 1)

            return carry

        lax.fori_loop(0, g_chunks + 1 - stage, finish, 0)
        return carry

    lax.fori_loop(0, 2, run_stage, 0)

    gain_remote().wait_send()
    w_remote().wait_send()
    for i in range(x_chunks):
        for way in range(3):
            x_remote(i, way).wait_send()

    @pl.when(has_later)
    def _():
        for stage in range(2):
            for i in range(x_chunks):
                halo_copy(stage, i).wait_send()

    @pl.when(has_earlier)
    def _():
        for stage in range(2):
            for h in range(heads):
                con_copy(stage, h).wait_send()

    for h in range(heads):
        swap_copy(1, h, core).wait_send()

    @pl.when(upper)
    def _():
        for h in range(heads):
            top_swap_copy(h, core).wait_send()
            down_copy(h).wait_send()

    @pl.when(lower)
    def _():
        for h in range(heads):
            swap_copy(0, h, core).wait_send()
            top_copy(h, side).wait_send()

    for stage in range(2):

        @pl.when(core + stage != 1)
        def _():
            for h in range(heads):
                out_partner(stage, h).wait_send()

        for h in range(heads):
            out_beside(stage, h).wait_send()

    for micro in range(2):
        for core_at in range(2):
            for h in range(heads):
                out_arrival(micro, core_at, h).wait()


def solution(mesh):
    pair_count = mesh.shape["ctx"] // 2

    def on_device(saved_inputs, scale_gains, out_proj, top_grad):
        _, micros, rows, features = saved_inputs.shape
        half_width = features // 2
        heads = half_width // HEAD_DIM
        x_chunks = heads // X_HEADS
        g_chunks = heads // G_HEADS
        dma = pltpu.SemaphoreType.DMA
        anywhere = pl.BlockSpec(memory_space=pl.ANY)
        result = pl.pallas_call(
            functools.partial(cascade_kernel, pair_count),
            out_shape=jax.ShapeDtypeStruct((micros, rows, features), BF16),
            in_specs=[anywhere] * 4,
            out_specs=anywhere,
            scratch_shapes=[
                pltpu.VMEM((2, 2 * rows, half_width), BF16),
                pltpu.VMEM((2, 2 * rows, half_width), BF16),
                pltpu.VMEM((2, 3, 1, half_width), F32),
                pltpu.VMEM((2, half_width, features), BF16),
                pltpu.VMEM((3, 2 * rows, features), BF16),
                pltpu.VMEM((2, heads, 4 * rows, HEAD_DIM), BF16),
                pltpu.VMEM((2, heads, 4 * rows, HEAD_DIM), BF16),
                pltpu.VMEM((2, heads, 2 * rows, HEAD_DIM), BF16),
                pltpu.VMEM((2, 2 * rows, half_width), F32),
                pltpu.VMEM((2, heads, 2, 2, rows, rows), F32),
                pltpu.VMEM((2, heads, 2, 3 * rows, rows), BF16),
                pltpu.VMEM((2 * rows, half_width), F32),
                pltpu.VMEM((2 * rows, half_width), F32),
                pltpu.VMEM((2, 2 * rows, half_width), BF16),
                pltpu.VMEM((2, 2 * rows, half_width), BF16),
                dma,
                dma((2,)),
                dma,
                dma((2,)),
                dma,
                dma((3, x_chunks)),
                dma((2, 2, x_chunks)),
                dma((2, x_chunks)),
                dma((2, x_chunks)),
                dma((2, heads)),
                dma((2, heads)),
                dma((2, heads)),
                dma((2, heads)),
                dma((heads,)),
                dma((heads,)),
                dma((2, 2, heads)),
                dma((2, 2, heads)),
            ],
            compiler_params=pltpu.CompilerParams(collective_id=0, has_side_effects=True),
        )(saved_inputs[0], scale_gains.reshape(3, 1, features), out_proj[0], top_grad)
        return result[None]

    return jax.shard_map(
        on_device,
        mesh=mesh,
        in_specs=(
            P("segment", None, "ctx", None),
            P("segment", None, None),
            P("segment", None, None),
            P(None, "ctx", None),
        ),
        out_specs=P("segment", None, "ctx", None),
        check_vma=False,
    )
```

```python
import functools

import jax
import jax.numpy as jnp
from jax import lax
from jax.experimental import pallas as pl
from jax.experimental.pallas import tpu as pltpu
from jax.sharding import PartitionSpec as P

HEAD_DIM = 128
X_HEADS = 1
G_HEADS = 2
QUERY_SCALE = 1.0 / 12.0
SOFT_CAP = 50.0
MESH = pl.DeviceIdType.MESH
F32 = jnp.float32
BF16 = jnp.bfloat16
NT = (((1,), (1,)), ((), ()))


def cols(at, width):
    return pl.ds(pl.multiple_of(at * width, width), width)


def dot_nt(a, b):
    return lax.dot_general(a, b, NT, preferred_element_type=F32)


def dot_nn(a, b):
    return jnp.dot(a, b, preferred_element_type=F32)


def cascade_kernel(
    pair_count,
    x_hbm,
    gain_hbm,
    w_hbm,
    top_hbm,
    out_hbm,
    x_own,
    x_halo,
    gains,
    w_buf,
    g_buf,
    v_all,
    kg_all,
    qg_all,
    o_all,
    slopes,
    weight_t,
    hg_sum,
    acc,
    con_send,
    con_recv,
    gain_send_sem,
    gain_sem,
    w_send_sem,
    w_sem,
    top_sem,
    x_send_sem,
    x_sem,
    halo_send_sem,
    halo_sem,
    con_send_sem,
    con_sem,
    swap_send_sem,
    swap_sem,
    cross_send_sem,
    cross_sem,
    out_send_sem,
    out_sem,
):
    rows = x_hbm.shape[1]
    features = x_hbm.shape[2]
    half_width = features // 2
    heads = half_width // HEAD_DIM
    x_width = X_HEADS * HEAD_DIM
    g_width = G_HEADS * HEAD_DIM
    x_chunks = half_width // x_width
    g_chunks = half_width // g_width

    seg = lax.axis_index("segment")
    ctx = lax.axis_index("ctx")
    half = seg // 2
    core = seg % 2
    pair = ctx // 2
    side = ctx % 2
    upper = half == 1
    lower = half == 0
    mine = jnp.where(upper, side, 1 - side)
    held = 1 - core
    has_later = pair < pair_count - 1
    has_earlier = pair > 0

    def place(half_at, core_at, pair_at, side_at):
        return (2 * half_at + core_at, 2 * pair_at + side_at)

    partner = place(half, 1 - core, pair, side)
    facing = place(1 - half, core, pair, 1 - side)
    later = place(half, core, jnp.minimum(pair + 1, pair_count - 1), side)
    earlier = place(half, core, jnp.maximum(pair - 1, 0), side)
    beside = place(half, core, pair, 1 - side)
    across = place(half, 1 - core, pair, 1 - side)

    def remote(src, dst, send_sem, recv_sem, device):
        return pltpu.make_async_remote_copy(
            src_ref=src,
            dst_ref=dst,
            send_sem=send_sem,
            recv_sem=recv_sem,
            device_id=device,
            device_id_type=MESH,
        )

    def gain_local():
        return pltpu.make_async_copy(
            gain_hbm.at[:, :, cols(core, half_width)], gains.at[held], gain_sem.at[held]
        )

    def gain_remote():
        return remote(
            gain_hbm.at[:, :, cols(1 - core, half_width)],
            gains.at[held],
            gain_send_sem,
            gain_sem.at[held],
            partner,
        )

    def gain_arrival(stage):
        return pltpu.make_async_copy(
            gain_hbm.at[:, :, cols(core, half_width)], gains.at[stage], gain_sem.at[stage]
        )

    def w_local():
        return pltpu.make_async_copy(
            w_hbm.at[cols(core, half_width), :], w_buf.at[held], w_sem.at[held]
        )

    def w_remote():
        return remote(
            w_hbm.at[cols(1 - core, half_width), :],
            w_buf.at[held],
            w_send_sem,
            w_sem.at[held],
            partner,
        )

    def w_arrival(stage):
        return pltpu.make_async_copy(
            w_hbm.at[cols(core, half_width), :], w_buf.at[stage], w_sem.at[stage]
        )

    def top_local():
        return pltpu.make_async_copy(
            top_hbm.at[mine], g_buf.at[0, cols(side, rows), :], top_sem
        )

    def x_local(i):
        return pltpu.make_async_copy(
            x_hbm.at[mine, :, cols(core * x_chunks + i, x_width)],
            x_own.at[held, cols(side, rows), cols(i, x_width)],
            x_sem.at[held, side, i],
        )

    def x_remote(i, way):
        micro = mine if way == 0 else 1 - mine
        core_at = core if way == 1 else 1 - core
        return remote(
            x_hbm.at[micro, :, cols(core_at * x_chunks + i, x_width)],
            x_own.at[held, cols(side, rows), cols(i, x_width)],
            x_send_sem.at[way, i],
            x_sem.at[held, side, i],
            (partner, beside, across)[way],
        )

    def x_arrival(stage, block, i):
        return pltpu.make_async_copy(
            x_hbm.at[mine, :, cols(core * x_chunks + i, x_width)],
            x_own.at[stage, cols(block, rows), cols(i, x_width)],
            x_sem.at[stage, block, i],
        )

    def halo_copy(stage, i):
        return remote(
            x_own.at[stage, :, cols(i, x_width)],
            x_halo.at[stage, :, cols(i, x_width)],
            halo_send_sem.at[stage, i],
            halo_sem.at[stage, i],
            later,
        )

    def con_copy(stage, h):
        return remote(
            con_send.at[stage, :, cols(h, HEAD_DIM)],
            con_recv.at[stage, :, cols(h, HEAD_DIM)],
            con_send_sem.at[stage, h],
            con_sem.at[stage, h],
            earlier,
        )

    def swap_copy(stage, h, core_at):
        ref = g_buf.at[stage, :, cols(core_at * heads + h, HEAD_DIM)]
        return remote(ref, ref, swap_send_sem.at[stage, h], swap_sem.at[stage, h], partner)

    def top_swap_copy(h, core_at):
        ref = g_buf.at[0, cols(1 - side, rows), cols(core_at * heads + h, HEAD_DIM)]
        return remote(ref, ref, swap_send_sem.at[0, h], swap_sem.at[0, h], partner)

    def down_copy(h):
        at = cols(core * heads + h, HEAD_DIM)
        return remote(
            g_buf.at[2, :, at], g_buf.at[0, :, at], cross_send_sem.at[h], cross_sem.at[h], facing
        )

    def top_copy(h, block):
        at = cols(core * heads + h, HEAD_DIM)
        return remote(
            top_hbm.at[mine, :, at],
            g_buf.at[0, cols(block, rows), at],
            cross_send_sem.at[h],
            cross_sem.at[h],
            facing,
        )

    def out_refs(stage, h, block):
        at = cols(core * heads + h, HEAD_DIM)
        return g_buf.at[stage + 1, cols(block, rows), at], out_hbm.at[mine, :, at]

    def out_local(stage, h):
        src, dst = out_refs(stage, h, side)
        return pltpu.make_async_copy(src, dst, out_sem.at[mine, core, h])

    def out_partner(stage, h):
        src, dst = out_refs(stage, h, side)
        return remote(
            src, dst, out_send_sem.at[stage, 0, h], out_sem.at[mine, core, h], partner
        )

    def out_beside(stage, h):
        src, dst = out_refs(stage, h, 1 - side)
        return remote(
            src,
            dst,
            out_send_sem.at[stage, 1, h],
            out_sem.at[mine, core, h],
            place(half, 1 - stage, pair, 1 - side),
        )

    def out_arrival(micro, core_at, h):
        at = cols(core_at * heads + h, HEAD_DIM)
        return pltpu.make_async_copy(
            g_buf.at[1, cols(0, rows), at], out_hbm.at[micro, :, at], out_sem.at[micro, core_at, h]
        )

    gain_local().start()
    for i in range(x_chunks):
        x_local(i).start()
    w_local().start()

    @pl.when(upper)
    def _():
        top_local().start()

    barrier = pltpu.get_barrier_semaphore()
    for peer in (partner, facing, beside, across):
        pl.semaphore_signal(barrier, inc=1, device_id=peer, device_id_type=MESH)

    @pl.when(has_later)
    def _():
        pl.semaphore_signal(barrier, inc=1, device_id=later, device_id_type=MESH)

    @pl.when(has_earlier)
    def _():
        pl.semaphore_signal(barrier, inc=1, device_id=earlier, device_id_type=MESH)

    @pl.when(jnp.logical_not(has_earlier))
    def _():
        x_halo[...] = jnp.zeros_like(x_halo)

    @pl.when(jnp.logical_not(has_later))
    def _():
        con_recv[...] = jnp.zeros_like(con_recv)

    peers = 4 + has_later.astype(jnp.int32) + has_earlier.astype(jnp.int32)
    pl.semaphore_wait(barrier, peers)

    def deliver():
        for i in range(x_chunks):
            for way in range(3):
                x_remote(i, way).start()

    @pl.when(core == 1)
    def _():
        deliver()

    gain_remote().start()

    @pl.when(lower)
    def _():
        for h in range(heads):
            top_copy(h, side).start()

    w_remote().start()

    def forward_one(stage, i):
        for block in range(2):
            x_arrival(stage, block, i).wait()

        @pl.when(has_later)
        def _():
            halo_copy(stage, i).start()

    def forward(stage):
        for i in range(x_chunks):
            forward_one(stage, i)

    forward(0)

    @pl.when(core == 0)
    def _():
        deliver()

    for stage in range(2):
        gain_arrival(stage).wait()

    row_at = lax.broadcasted_iota(jnp.int32, (rows, rows), 0)
    col_at = lax.broadcasted_iota(jnp.int32, (rows, rows), 1)
    own = col_at <= row_at
    seen = (pair >= 1).astype(F32)

    def prepare_head(stage, h):
        at = cols(h, HEAD_DIM)
        gq, gk, gv = (gains[stage, n, :, at] for n in range(3))
        x = jnp.concatenate([x_halo[stage, :, at], x_own[stage, :, at]], axis=0).astype(F32)
        q = (x[2 * rows :] * gq).astype(BF16)
        k = (x * gk).astype(BF16)
        v = (x * gv).astype(BF16)
        v_all[stage, h] = v
        kg_all[stage, h] = (k.astype(F32) * gq).astype(BF16)
        qg_all[stage, h] = (q.astype(F32) * gk).astype(BF16)
        for block in range(2):
            low = block * rows
            span = slice(low, low + 3 * rows)
            s = dot_nt(q[low : low + rows], k[span]) * (QUERY_SCALE / SOFT_CAP)
            t_one = jnp.tanh(s[:, rows : 2 * rows])
            t_mix = jnp.tanh(jnp.where(own, s[:, 2 * rows :], s[:, :rows]))
            e_one = jnp.exp(SOFT_CAP * t_one)
            if block == 0:
                e_one = e_one * seen
            e_mix = jnp.exp(SOFT_CAP * t_mix)
            e_mix = jnp.where(own, e_mix, e_mix * seen)
            scale = 1.0 / jnp.sum(e_one + e_mix, axis=1, keepdims=True)
            w_one = e_one * scale
            w_mix = e_mix * scale
            slopes[stage, h, block, 0] = w_one * (1.0 - t_one * t_one) * QUERY_SCALE
            slopes[stage, h, block, 1] = w_mix * (1.0 - t_mix * t_mix) * QUERY_SCALE
            w_cat = jnp.concatenate(
                [jnp.where(own, 0.0, w_mix), w_one, jnp.where(own, w_mix, 0.0)], axis=1
            ).astype(BF16)
            o_all[stage, low : low + rows, at] = dot_nn(w_cat, v[span])
            weight_t[stage, h, block] = w_cat.T

    def attend_head(stage, h):
        at = cols(h, HEAD_DIM)
        gv = gains[stage, 2, :, at]
        both = []
        d_query = []
        for block in range(2):
            low = block * rows
            hg = hg_sum[low : low + rows, at].astype(BF16)
            hg_f = hg.astype(F32)
            gw = dot_nt(hg, v_all[stage, h, low : low + 3 * rows])
            row_dot = jnp.sum(hg_f * o_all[stage, low : low + rows, at], axis=1, keepdims=True)
            d_one = slopes[stage, h, block, 0] * (gw[:, rows : 2 * rows] - row_dot)
            d_mix = slopes[stage, h, block, 1] * (
                jnp.where(own, gw[:, 2 * rows :], gw[:, :rows]) - row_dot
            )
            d_cat = jnp.concatenate(
                [jnp.where(own, 0.0, d_mix), d_one, jnp.where(own, d_mix, 0.0)], axis=1
            ).astype(BF16)
            d_t = d_cat.T
            left = jnp.concatenate([d_t, weight_t[stage, h, block]], axis=1)
            right = jnp.concatenate(
                [qg_all[stage, h, low : low + rows], (hg_f * gv).astype(BF16)], axis=0
            )
            both.append(dot_nn(left, right))
            d_query.append(dot_nn(d_cat, kg_all[stage, h, low : low + 3 * rows]))
        con_send[stage, :rows, at] = both[0][:rows].astype(BF16)
        con_send[stage, rows:, at] = (both[0][rows : 2 * rows] + both[1][:rows]).astype(BF16)
        g_at = cols(core * heads + h, HEAD_DIM)
        acc[:rows, at] = (
            g_buf[stage, :rows, g_at].astype(F32)
            + d_query[0]
            + both[0][2 * rows :]
            + both[1][rows : 2 * rows]
        )
        acc[rows:, at] = (
            g_buf[stage, rows:, g_at].astype(F32) + d_query[1] + both[1][2 * rows :]
        )

    def ready_head(stage, h):
        @pl.when(has_earlier)
        def _():
            halo_copy(stage, h).wait_recv()

        prepare_head(stage, h)

    def absorb(stage, k):
        at = cols(k, g_width)
        hg_sum[...] += dot_nt(g_buf[stage, :, at], w_buf[stage, :, at])

    def absorb_partner(stage, f):
        for j in range(G_HEADS):
            swap_copy(stage, f * G_HEADS + j, 1 - core).wait_recv()
        absorb(stage, (1 - core) * g_chunks + f)

    @pl.when(lower)
    def _():
        forward(1)

        def ahead(n, carry):
            ready_head(n // heads, n % heads)
            return carry

        lax.fori_loop(0, 2 * heads, ahead, 0)

    hg_sum[...] = jnp.zeros_like(hg_sum)
    w_arrival(0).wait()

    @pl.when(upper)
    def _():
        top_local().wait()
        for h in range(heads):
            top_copy(h, 1 - side).wait_recv()
            top_swap_copy(h, core).start()

        def take(f, carry):
            absorb(0, core * g_chunks + f)
            for j in range(G_HEADS):
                top_swap_copy(f * G_HEADS + j, 1 - core).wait_recv()
            absorb(0, (1 - core) * g_chunks + f)
            return carry

        lax.fori_loop(0, g_chunks, take, 0)
        ready_head(0, 0)

    @pl.when(lower)
    def _():
        def take(f, carry):
            @pl.when(f < g_chunks)
            def _():
                for j in range(G_HEADS):
                    down_copy(f * G_HEADS + j).wait_recv()
                    swap_copy(0, f * G_HEADS + j, core).start()
                absorb(0, core * g_chunks + f)

            @pl.when(f > 0)
            def _():
                absorb_partner(0, f - 1)

            return carry

        lax.fori_loop(0, g_chunks + 1, take, 0)

    def run_stage(stage, carry):
        def send(h):
            @pl.when(has_earlier)
            def _():
                con_copy(stage, h).start()

        def attend(h, carry):
            attend_head(stage, h)
            send(h)
            return carry

        def attend_ahead(h, carry):
            @pl.when(has_earlier)
            def _():
                halo_copy(stage, h + 1).wait_recv()

            attend_head(stage, h)
            prepare_head(stage, h + 1)
            send(h)

            @pl.when((stage == 0) & (h >= 0))
            def _():
                forward_one(1, h - 0)

            @pl.when((stage == 0) & (h == heads - 2))
            def _():
                for i in range(x_chunks - 1, x_chunks):
                    forward_one(1, i)

            return carry

        @pl.when(upper)
        def _():
            lax.fori_loop(0, heads - 1, attend_ahead, 0)

        lax.fori_loop(jnp.where(upper, heads - 1, 0), heads, attend, 0)

        @pl.when(upper & (stage == 0))
        def _():
            ready_head(1, 0)

        @pl.when(stage == 0)
        def _():
            hg_sum[...] = jnp.zeros_like(hg_sum)
            w_arrival(1).wait()

        def finish(f, carry):
            @pl.when(f < g_chunks)
            def _():
                for j in range(G_HEADS):
                    h = f * G_HEADS + j

                    @pl.when(has_later)
                    def _():
                        con_copy(stage, h).wait_recv()

                    at = cols(h, HEAD_DIM)
                    total = acc[:, at] + con_recv[stage, :, at].astype(F32)
                    g_buf[stage + 1, :, cols(core * heads + h, HEAD_DIM)] = total.astype(BF16)

                    @pl.when(stage == 0)
                    def _():
                        swap_copy(1, h, core).start()

                    @pl.when((stage == 1) & upper)
                    def _():
                        down_copy(h).start()

                    out_beside(stage, h).start()

                    @pl.when(core + stage == 1)
                    def _():
                        out_local(stage, h).start()

                    @pl.when(core + stage != 1)
                    def _():
                        out_partner(stage, h).start()

                @pl.when(stage == 0)
                def _():
                    absorb(1, core * g_chunks + f)

            @pl.when((stage == 0) & (f > 0))
            def _():
                absorb_partner(1, f - 1)

            return carry

        lax.fori_loop(0, g_chunks + 1 - stage, finish, 0)
        return carry

    lax.fori_loop(0, 2, run_stage, 0)

    gain_remote().wait_send()
    w_remote().wait_send()
    for i in range(x_chunks):
        for way in range(3):
            x_remote(i, way).wait_send()

    @pl.when(has_later)
    def _():
        for stage in range(2):
            for i in range(x_chunks):
                halo_copy(stage, i).wait_send()

    @pl.when(has_earlier)
    def _():
        for stage in range(2):
            for h in range(heads):
                con_copy(stage, h).wait_send()

    for h in range(heads):
        swap_copy(1, h, core).wait_send()

    @pl.when(upper)
    def _():
        for h in range(heads):
            top_swap_copy(h, core).wait_send()
            down_copy(h).wait_send()

    @pl.when(lower)
    def _():
        for h in range(heads):
            swap_copy(0, h, core).wait_send()
            top_copy(h, side).wait_send()

    for stage in range(2):

        @pl.when(core + stage != 1)
        def _():
            for h in range(heads):
                out_partner(stage, h).wait_send()

        for h in range(heads):
            out_beside(stage, h).wait_send()

    for micro in range(2):
        for core_at in range(2):
            for h in range(heads):
                out_arrival(micro, core_at, h).wait()


def solution(mesh):
    pair_count = mesh.shape["ctx"] // 2

    def on_device(saved_inputs, scale_gains, out_proj, top_grad):
        _, micros, rows, features = saved_inputs.shape
        half_width = features // 2
        heads = half_width // HEAD_DIM
        x_chunks = heads // X_HEADS
        g_chunks = heads // G_HEADS
        dma = pltpu.SemaphoreType.DMA
        anywhere = pl.BlockSpec(memory_space=pl.ANY)
        result = pl.pallas_call(
            functools.partial(cascade_kernel, pair_count),
            out_shape=jax.ShapeDtypeStruct((micros, rows, features), BF16),
            in_specs=[anywhere] * 4,
            out_specs=anywhere,
            scratch_shapes=[
                pltpu.VMEM((2, 2 * rows, half_width), BF16),
                pltpu.VMEM((2, 2 * rows, half_width), BF16),
                pltpu.VMEM((2, 3, 1, half_width), F32),
                pltpu.VMEM((2, half_width, features), BF16),
                pltpu.VMEM((3, 2 * rows, features), BF16),
                pltpu.VMEM((2, heads, 4 * rows, HEAD_DIM), BF16),
                pltpu.VMEM((2, heads, 4 * rows, HEAD_DIM), BF16),
                pltpu.VMEM((2, heads, 2 * rows, HEAD_DIM), BF16),
                pltpu.VMEM((2, 2 * rows, half_width), F32),
                pltpu.VMEM((2, heads, 2, 2, rows, rows), F32),
                pltpu.VMEM((2, heads, 2, 3 * rows, rows), BF16),
                pltpu.VMEM((2 * rows, half_width), F32),
                pltpu.VMEM((2 * rows, half_width), F32),
                pltpu.VMEM((2, 2 * rows, half_width), BF16),
                pltpu.VMEM((2, 2 * rows, half_width), BF16),
                dma,
                dma((2,)),
                dma,
                dma((2,)),
                dma,
                dma((3, x_chunks)),
                dma((2, 2, x_chunks)),
                dma((2, x_chunks)),
                dma((2, x_chunks)),
                dma((2, heads)),
                dma((2, heads)),
                dma((2, heads)),
                dma((2, heads)),
                dma((heads,)),
                dma((heads,)),
                dma((2, 2, heads)),
                dma((2, 2, heads)),
            ],
            compiler_params=pltpu.CompilerParams(collective_id=0, has_side_effects=True),
        )(saved_inputs[0], scale_gains.reshape(3, 1, features), out_proj[0], top_grad)
        return result[None]

    return jax.shard_map(
        on_device,
        mesh=mesh,
        in_specs=(
            P("segment", None, "ctx", None),
            P("segment", None, None),
            P("segment", None, None),
            P(None, "ctx", None),
        ),
        out_specs=P("segment", None, "ctx", None),
        check_vma=False,
    )
```

```python
import functools

import jax
import jax.numpy as jnp
from jax import lax
from jax.experimental import pallas as pl
from jax.experimental.pallas import tpu as pltpu
from jax.sharding import PartitionSpec as P

HEAD_DIM = 128
X_HEADS = 1
G_HEADS = 2
QUERY_SCALE = 1.0 / 12.0
SOFT_CAP = 50.0
MESH = pl.DeviceIdType.MESH
F32 = jnp.float32
BF16 = jnp.bfloat16
NT = (((1,), (1,)), ((), ()))


def cols(at, width):
    return pl.ds(pl.multiple_of(at * width, width), width)


def dot_nt(a, b):
    return lax.dot_general(a, b, NT, preferred_element_type=F32)


def dot_nn(a, b):
    return jnp.dot(a, b, preferred_element_type=F32)


def cascade_kernel(
    pair_count,
    x_hbm,
    gain_hbm,
    w_hbm,
    top_hbm,
    out_hbm,
    x_own,
    x_halo,
    gains,
    w_buf,
    g_buf,
    v_all,
    kg_all,
    qg_all,
    o_all,
    slopes,
    weight_t,
    hg_sum,
    acc,
    con_send,
    con_recv,
    gain_send_sem,
    gain_sem,
    w_send_sem,
    w_sem,
    top_sem,
    x_send_sem,
    x_sem,
    halo_send_sem,
    halo_sem,
    con_send_sem,
    con_sem,
    swap_send_sem,
    swap_sem,
    cross_send_sem,
    cross_sem,
    out_send_sem,
    out_sem,
):
    rows = x_hbm.shape[1]
    features = x_hbm.shape[2]
    half_width = features // 2
    heads = half_width // HEAD_DIM
    x_width = X_HEADS * HEAD_DIM
    g_width = G_HEADS * HEAD_DIM
    x_chunks = half_width // x_width
    g_chunks = half_width // g_width

    seg = lax.axis_index("segment")
    ctx = lax.axis_index("ctx")
    half = seg // 2
    core = seg % 2
    pair = ctx // 2
    side = ctx % 2
    upper = half == 1
    lower = half == 0
    mine = jnp.where(upper, side, 1 - side)
    held = 1 - core
    has_later = pair < pair_count - 1
    has_earlier = pair > 0

    def place(half_at, core_at, pair_at, side_at):
        return (2 * half_at + core_at, 2 * pair_at + side_at)

    partner = place(half, 1 - core, pair, side)
    facing = place(1 - half, core, pair, 1 - side)
    later = place(half, core, jnp.minimum(pair + 1, pair_count - 1), side)
    earlier = place(half, core, jnp.maximum(pair - 1, 0), side)
    beside = place(half, core, pair, 1 - side)
    across = place(half, 1 - core, pair, 1 - side)

    def remote(src, dst, send_sem, recv_sem, device):
        return pltpu.make_async_remote_copy(
            src_ref=src,
            dst_ref=dst,
            send_sem=send_sem,
            recv_sem=recv_sem,
            device_id=device,
            device_id_type=MESH,
        )

    def gain_local():
        return pltpu.make_async_copy(
            gain_hbm.at[:, :, cols(core, half_width)], gains.at[held], gain_sem.at[held]
        )

    def gain_remote():
        return remote(
            gain_hbm.at[:, :, cols(1 - core, half_width)],
            gains.at[held],
            gain_send_sem,
            gain_sem.at[held],
            partner,
        )

    def gain_arrival(stage):
        return pltpu.make_async_copy(
            gain_hbm.at[:, :, cols(core, half_width)], gains.at[stage], gain_sem.at[stage]
        )

    def w_local():
        return pltpu.make_async_copy(
            w_hbm.at[cols(core, half_width), :], w_buf.at[held], w_sem.at[held]
        )

    def w_remote():
        return remote(
            w_hbm.at[cols(1 - core, half_width), :],
            w_buf.at[held],
            w_send_sem,
            w_sem.at[held],
            partner,
        )

    def w_arrival(stage):
        return pltpu.make_async_copy(
            w_hbm.at[cols(core, half_width), :], w_buf.at[stage], w_sem.at[stage]
        )

    def top_local():
        return pltpu.make_async_copy(
            top_hbm.at[mine], g_buf.at[0, cols(side, rows), :], top_sem
        )

    def x_local(i):
        return pltpu.make_async_copy(
            x_hbm.at[mine, :, cols(core * x_chunks + i, x_width)],
            x_own.at[held, cols(side, rows), cols(i, x_width)],
            x_sem.at[held, side, i],
        )

    def x_remote(i, way):
        micro = mine if way == 0 else 1 - mine
        core_at = core if way == 1 else 1 - core
        return remote(
            x_hbm.at[micro, :, cols(core_at * x_chunks + i, x_width)],
            x_own.at[held, cols(side, rows), cols(i, x_width)],
            x_send_sem.at[way, i],
            x_sem.at[held, side, i],
            (partner, beside, across)[way],
        )

    def x_arrival(stage, block, i):
        return pltpu.make_async_copy(
            x_hbm.at[mine, :, cols(core * x_chunks + i, x_width)],
            x_own.at[stage, cols(block, rows), cols(i, x_width)],
            x_sem.at[stage, block, i],
        )

    def halo_copy(stage, i):
        return remote(
            x_own.at[stage, :, cols(i, x_width)],
            x_halo.at[stage, :, cols(i, x_width)],
            halo_send_sem.at[stage, i],
            halo_sem.at[stage, i],
            later,
        )

    def con_copy(stage, h):
        return remote(
            con_send.at[stage, :, cols(h, HEAD_DIM)],
            con_recv.at[stage, :, cols(h, HEAD_DIM)],
            con_send_sem.at[stage, h],
            con_sem.at[stage, h],
            earlier,
        )

    def swap_copy(stage, h, core_at):
        ref = g_buf.at[stage, :, cols(core_at * heads + h, HEAD_DIM)]
        return remote(ref, ref, swap_send_sem.at[stage, h], swap_sem.at[stage, h], partner)

    def top_swap_copy(h, core_at):
        ref = g_buf.at[0, cols(1 - side, rows), cols(core_at * heads + h, HEAD_DIM)]
        return remote(ref, ref, swap_send_sem.at[0, h], swap_sem.at[0, h], partner)

    def down_copy(h):
        at = cols(core * heads + h, HEAD_DIM)
        return remote(
            g_buf.at[2, :, at], g_buf.at[0, :, at], cross_send_sem.at[h], cross_sem.at[h], facing
        )

    def top_copy(h, block):
        at = cols(core * heads + h, HEAD_DIM)
        return remote(
            top_hbm.at[mine, :, at],
            g_buf.at[0, cols(block, rows), at],
            cross_send_sem.at[h],
            cross_sem.at[h],
            facing,
        )

    def out_refs(stage, h, block):
        at = cols(core * heads + h, HEAD_DIM)
        return g_buf.at[stage + 1, cols(block, rows), at], out_hbm.at[mine, :, at]

    def out_local(stage, h):
        src, dst = out_refs(stage, h, side)
        return pltpu.make_async_copy(src, dst, out_sem.at[mine, core, h])

    def out_partner(stage, h):
        src, dst = out_refs(stage, h, side)
        return remote(
            src, dst, out_send_sem.at[stage, 0, h], out_sem.at[mine, core, h], partner
        )

    def out_beside(stage, h):
        src, dst = out_refs(stage, h, 1 - side)
        return remote(
            src,
            dst,
            out_send_sem.at[stage, 1, h],
            out_sem.at[mine, core, h],
            place(half, 1 - stage, pair, 1 - side),
        )

    def out_arrival(micro, core_at, h):
        at = cols(core_at * heads + h, HEAD_DIM)
        return pltpu.make_async_copy(
            g_buf.at[1, cols(0, rows), at], out_hbm.at[micro, :, at], out_sem.at[micro, core_at, h]
        )

    gain_local().start()
    for i in range(x_chunks):
        x_local(i).start()
    w_local().start()

    @pl.when(upper)
    def _():
        top_local().start()

    barrier = pltpu.get_barrier_semaphore()
    for peer in (partner, facing, beside, across):
        pl.semaphore_signal(barrier, inc=1, device_id=peer, device_id_type=MESH)

    @pl.when(has_later)
    def _():
        pl.semaphore_signal(barrier, inc=1, device_id=later, device_id_type=MESH)

    @pl.when(has_earlier)
    def _():
        pl.semaphore_signal(barrier, inc=1, device_id=earlier, device_id_type=MESH)

    @pl.when(jnp.logical_not(has_earlier))
    def _():
        x_halo[...] = jnp.zeros_like(x_halo)

    @pl.when(jnp.logical_not(has_later))
    def _():
        con_recv[...] = jnp.zeros_like(con_recv)

    peers = 4 + has_later.astype(jnp.int32) + has_earlier.astype(jnp.int32)
    pl.semaphore_wait(barrier, peers)

    def deliver():
        for i in range(x_chunks):
            for way in range(3):
                x_remote(i, way).start()

    @pl.when(core == 1)
    def _():
        deliver()

    gain_remote().start()

    @pl.when(lower)
    def _():
        for h in range(heads):
            top_copy(h, side).start()

    w_remote().start()

    def forward_one(stage, i):
        for block in range(2):
            x_arrival(stage, block, i).wait()

        @pl.when(has_later)
        def _():
            halo_copy(stage, i).start()

    def forward(stage):
        for i in range(x_chunks):
            forward_one(stage, i)

    forward(0)

    @pl.when(core == 0)
    def _():
        deliver()

    for stage in range(2):
        gain_arrival(stage).wait()

    row_at = lax.broadcasted_iota(jnp.int32, (rows, rows), 0)
    col_at = lax.broadcasted_iota(jnp.int32, (rows, rows), 1)
    own = col_at <= row_at
    seen = (pair >= 1).astype(F32)

    def prepare_head(stage, h):
        at = cols(h, HEAD_DIM)
        gq, gk, gv = (gains[stage, n, :, at] for n in range(3))
        x = jnp.concatenate([x_halo[stage, :, at], x_own[stage, :, at]], axis=0).astype(F32)
        q = (x[2 * rows :] * gq).astype(BF16)
        k = (x * gk).astype(BF16)
        v = (x * gv).astype(BF16)
        v_all[stage, h] = v
        kg_all[stage, h] = (k.astype(F32) * gq).astype(BF16)
        qg_all[stage, h] = (q.astype(F32) * gk).astype(BF16)
        for block in range(2):
            low = block * rows
            span = slice(low, low + 3 * rows)
            s = dot_nt(q[low : low + rows], k[span]) * (QUERY_SCALE / SOFT_CAP)
            t_one = jnp.tanh(s[:, rows : 2 * rows])
            t_mix = jnp.tanh(jnp.where(own, s[:, 2 * rows :], s[:, :rows]))
            e_one = jnp.exp(SOFT_CAP * t_one)
            if block == 0:
                e_one = e_one * seen
            e_mix = jnp.exp(SOFT_CAP * t_mix)
            e_mix = jnp.where(own, e_mix, e_mix * seen)
            scale = 1.0 / jnp.sum(e_one + e_mix, axis=1, keepdims=True)
            w_one = e_one * scale
            w_mix = e_mix * scale
            slopes[stage, h, block, 0] = w_one * (1.0 - t_one * t_one) * QUERY_SCALE
            slopes[stage, h, block, 1] = w_mix * (1.0 - t_mix * t_mix) * QUERY_SCALE
            w_cat = jnp.concatenate(
                [jnp.where(own, 0.0, w_mix), w_one, jnp.where(own, w_mix, 0.0)], axis=1
            ).astype(BF16)
            o_all[stage, low : low + rows, at] = dot_nn(w_cat, v[span])
            weight_t[stage, h, block] = w_cat.T

    def attend_head(stage, h):
        at = cols(h, HEAD_DIM)
        gv = gains[stage, 2, :, at]
        both = []
        d_query = []
        for block in range(2):
            low = block * rows
            hg = hg_sum[low : low + rows, at].astype(BF16)
            hg_f = hg.astype(F32)
            gw = dot_nt(hg, v_all[stage, h, low : low + 3 * rows])
            row_dot = jnp.sum(hg_f * o_all[stage, low : low + rows, at], axis=1, keepdims=True)
            d_one = slopes[stage, h, block, 0] * (gw[:, rows : 2 * rows] - row_dot)
            d_mix = slopes[stage, h, block, 1] * (
                jnp.where(own, gw[:, 2 * rows :], gw[:, :rows]) - row_dot
            )
            d_cat = jnp.concatenate(
                [jnp.where(own, 0.0, d_mix), d_one, jnp.where(own, d_mix, 0.0)], axis=1
            ).astype(BF16)
            d_t = d_cat.T
            left = jnp.concatenate([d_t, weight_t[stage, h, block]], axis=1)
            right = jnp.concatenate(
                [qg_all[stage, h, low : low + rows], (hg_f * gv).astype(BF16)], axis=0
            )
            both.append(dot_nn(left, right))
            d_query.append(dot_nn(d_cat, kg_all[stage, h, low : low + 3 * rows]))
        con_send[stage, :rows, at] = both[0][:rows].astype(BF16)
        con_send[stage, rows:, at] = (both[0][rows : 2 * rows] + both[1][:rows]).astype(BF16)
        g_at = cols(core * heads + h, HEAD_DIM)
        acc[:rows, at] = (
            g_buf[stage, :rows, g_at].astype(F32)
            + d_query[0]
            + both[0][2 * rows :]
            + both[1][rows : 2 * rows]
        )
        acc[rows:, at] = (
            g_buf[stage, rows:, g_at].astype(F32) + d_query[1] + both[1][2 * rows :]
        )

    def ready_head(stage, h):
        @pl.when(has_earlier)
        def _():
            halo_copy(stage, h).wait_recv()

        prepare_head(stage, h)

    def absorb(stage, k):
        at = cols(k, g_width)
        hg_sum[...] += dot_nt(g_buf[stage, :, at], w_buf[stage, :, at])

    def absorb_partner(stage, f):
        for j in range(G_HEADS):
            swap_copy(stage, f * G_HEADS + j, 1 - core).wait_recv()
        absorb(stage, (1 - core) * g_chunks + f)

    @pl.when(lower)
    def _():
        forward(1)

        def ahead(n, carry):
            ready_head(n // heads, n % heads)
            return carry

        lax.fori_loop(0, 2 * heads, ahead, 0)

    hg_sum[...] = jnp.zeros_like(hg_sum)
    w_arrival(0).wait()

    @pl.when(upper)
    def _():
        top_local().wait()
        for h in range(heads):
            top_copy(h, 1 - side).wait_recv()
            top_swap_copy(h, core).start()

        def take(f, carry):
            absorb(0, core * g_chunks + f)
            for j in range(G_HEADS):
                top_swap_copy(f * G_HEADS + j, 1 - core).wait_recv()
            absorb(0, (1 - core) * g_chunks + f)
            return carry

        lax.fori_loop(0, g_chunks, take, 0)
        ready_head(0, 0)

    @pl.when(lower)
    def _():
        def take(f, carry):
            @pl.when(f < g_chunks)
            def _():
                for j in range(G_HEADS):
                    down_copy(f * G_HEADS + j).wait_recv()
                    swap_copy(0, f * G_HEADS + j, core).start()
                absorb(0, core * g_chunks + f)

            @pl.when(f > 0)
            def _():
                absorb_partner(0, f - 1)

            return carry

        lax.fori_loop(0, g_chunks + 1, take, 0)

    def run_stage(stage, carry):
        def send(h):
            @pl.when(has_earlier)
            def _():
                con_copy(stage, h).start()

        def attend(h, carry):
            attend_head(stage, h)
            send(h)
            return carry

        def attend_ahead(h, carry):
            @pl.when(has_earlier)
            def _():
                halo_copy(stage, h + 1).wait_recv()

            attend_head(stage, h)
            prepare_head(stage, h + 1)
            send(h)

            @pl.when((stage == 0) & (h >= 0))
            def _():
                forward_one(1, h - 0)

            @pl.when((stage == 0) & (h == heads - 2))
            def _():
                for i in range(x_chunks - 1, x_chunks):
                    forward_one(1, i)

            return carry

        @pl.when(upper)
        def _():
            lax.fori_loop(0, heads - 1, attend_ahead, 0)

        lax.fori_loop(jnp.where(upper, heads - 1, 0), heads, attend, 0)

        @pl.when(upper & (stage == 0))
        def _():
            ready_head(1, 0)

        @pl.when(stage == 0)
        def _():
            hg_sum[...] = jnp.zeros_like(hg_sum)
            w_arrival(1).wait()

        def finish(f, carry):
            @pl.when(f < g_chunks)
            def _():
                for j in range(G_HEADS):
                    h = f * G_HEADS + j

                    @pl.when(has_later)
                    def _():
                        con_copy(stage, h).wait_recv()

                    at = cols(h, HEAD_DIM)
                    total = acc[:, at] + con_recv[stage, :, at].astype(F32)
                    g_buf[stage + 1, :, cols(core * heads + h, HEAD_DIM)] = total.astype(BF16)

                    @pl.when(stage == 0)
                    def _():
                        swap_copy(1, h, core).start()

                    @pl.when((stage == 1) & upper)
                    def _():
                        down_copy(h).start()

                    out_beside(stage, h).start()

                    @pl.when(core + stage == 1)
                    def _():
                        out_local(stage, h).start()

                    @pl.when(core + stage != 1)
                    def _():
                        out_partner(stage, h).start()

                @pl.when(stage == 0)
                def _():
                    absorb(1, core * g_chunks + f)

            @pl.when((stage == 0) & (f > 0))
            def _():
                absorb_partner(1, f - 1)

            return carry

        lax.fori_loop(0, g_chunks + 1 - stage, finish, 0)
        return carry

    lax.fori_loop(0, 2, run_stage, 0)

    gain_remote().wait_send()
    w_remote().wait_send()
    for i in range(x_chunks):
        for way in range(3):
            x_remote(i, way).wait_send()

    @pl.when(has_later)
    def _():
        for stage in range(2):
            for i in range(x_chunks):
                halo_copy(stage, i).wait_send()

    @pl.when(has_earlier)
    def _():
        for stage in range(2):
            for h in range(heads):
                con_copy(stage, h).wait_send()

    for h in range(heads):
        swap_copy(1, h, core).wait_send()

    @pl.when(upper)
    def _():
        for h in range(heads):
            top_swap_copy(h, core).wait_send()
            down_copy(h).wait_send()

    @pl.when(lower)
    def _():
        for h in range(heads):
            swap_copy(0, h, core).wait_send()
            top_copy(h, side).wait_send()

    for stage in range(2):

        @pl.when(core + stage != 1)
        def _():
            for h in range(heads):
                out_partner(stage, h).wait_send()

        for h in range(heads):
            out_beside(stage, h).wait_send()

    for micro in range(2):
        for core_at in range(2):
            for h in range(heads):
                out_arrival(micro, core_at, h).wait()


def hand_on_kernel(parts, in_hbm, out_hbm, held, in_sem, out_sem):
    rows = in_hbm.shape[1] // (parts // 2)

    def piece(ref, n):
        return ref.at[n // (parts // 2), pl.ds((n % (parts // 2)) * rows, rows), :]

    def load(n):
        return pltpu.make_async_copy(piece(in_hbm, n), held.at[n], in_sem.at[n])

    def store(n):
        return pltpu.make_async_copy(held.at[n], piece(out_hbm, n), out_sem.at[n])

    for n in range(parts):
        load(n).start()
    for n in range(parts):
        load(n).wait()
        store(n).start()
    for n in range(parts):
        store(n).wait()


def solution(mesh):
    pair_count = mesh.shape["ctx"] // 2

    def on_device(saved_inputs, scale_gains, out_proj, top_grad):
        _, micros, rows, features = saved_inputs.shape
        half_width = features // 2
        heads = half_width // HEAD_DIM
        x_chunks = heads // X_HEADS
        g_chunks = heads // G_HEADS
        dma = pltpu.SemaphoreType.DMA
        anywhere = pl.BlockSpec(memory_space=pl.ANY)
        result = pl.pallas_call(
            functools.partial(cascade_kernel, pair_count),
            out_shape=jax.ShapeDtypeStruct((micros, rows, features), BF16),
            in_specs=[anywhere] * 4,
            out_specs=anywhere,
            scratch_shapes=[
                pltpu.VMEM((2, 2 * rows, half_width), BF16),
                pltpu.VMEM((2, 2 * rows, half_width), BF16),
                pltpu.VMEM((2, 3, 1, half_width), F32),
                pltpu.VMEM((2, half_width, features), BF16),
                pltpu.VMEM((3, 2 * rows, features), BF16),
                pltpu.VMEM((2, heads, 4 * rows, HEAD_DIM), BF16),
                pltpu.VMEM((2, heads, 4 * rows, HEAD_DIM), BF16),
                pltpu.VMEM((2, heads, 2 * rows, HEAD_DIM), BF16),
                pltpu.VMEM((2, 2 * rows, half_width), F32),
                pltpu.VMEM((2, heads, 2, 2, rows, rows), F32),
                pltpu.VMEM((2, heads, 2, 3 * rows, rows), BF16),
                pltpu.VMEM((2 * rows, half_width), F32),
                pltpu.VMEM((2 * rows, half_width), F32),
                pltpu.VMEM((2, 2 * rows, half_width), BF16),
                pltpu.VMEM((2, 2 * rows, half_width), BF16),
                dma,
                dma((2,)),
                dma,
                dma((2,)),
                dma,
                dma((3, x_chunks)),
                dma((2, 2, x_chunks)),
                dma((2, x_chunks)),
                dma((2, x_chunks)),
                dma((2, heads)),
                dma((2, heads)),
                dma((2, heads)),
                dma((2, heads)),
                dma((heads,)),
                dma((heads,)),
                dma((2, 2, heads)),
                dma((2, 2, heads)),
            ],
            compiler_params=pltpu.CompilerParams(collective_id=0, has_side_effects=True),
        )(saved_inputs[0], scale_gains.reshape(3, 1, features), out_proj[0], top_grad)
        parts = 8
        result = pl.pallas_call(
            functools.partial(hand_on_kernel, parts),
            out_shape=jax.ShapeDtypeStruct(result.shape, BF16),
            in_specs=[anywhere],
            out_specs=anywhere,
            scratch_shapes=[
                pltpu.VMEM((parts, micros * rows // parts, features), BF16),
                dma((parts,)),
                dma((parts,)),
            ],
        )(result)
        return result[None]

    return jax.shard_map(
        on_device,
        mesh=mesh,
        in_specs=(
            P("segment", None, "ctx", None),
            P("segment", None, None),
            P("segment", None, None),
            P(None, "ctx", None),
        ),
        out_specs=P("segment", None, "ctx", None),
        check_vma=False,
    )
```
